128 devices in a mesh: grp: 8 (over x, y_hi), dev: 16 (over y_lo, z, core).
Axes of the slice: x: 4, y: 4 (y_hi: 2, y_lo: 2; y = y_hi * 2 + y_lo), z: 4, core: 2. Of those that a mesh axis runs over, the one named last changes fastest.
Arguments:
- batch_rows: bfloat16 [4096, 512], P(('grp', 'dev')), may hold values from -30 to 30
- batch_labels: int32 [4096], P(('grp', 'dev')), may hold values from 0 to 1023, as said below
- memory: bfloat16 [262144, 512], P(('grp', 'dev')), may hold values from -30 to 30
- memory_labels: int32 [262144], P(('grp', 'dev')), may hold values from 0 to 1023
- keep_bits: int32 [262144], P(('grp', 'dev')), may hold values from 0 to 1
- step_index: int32 [1], replicated, may hold values from 0 to 999999
Outputs:
- grad_batch: float32 [4096, 512], P(('grp', 'dev'))
- anchor_loss: float32 [4096], P(('grp', 'dev'))
- new_memory: bfloat16 [262144, 512], P(('grp', 'dev'))
- new_labels: int32 [262144], P(('grp', 'dev'))
The draws below stay inside these ranges and needn't reach their ends.
Inputs may be any that keep to these rules, and one draw needn't show every extreme that they name: `batch_labels`: labels of batch and memory rows are class numbers below 1024.
All inputs are finite; a program needn't handle non-finite values.
Results may differ from the reference program's by a relative error of at most 0.0034.
Values may be sent and summed in bfloat16 or wider, within the bound.
A program may use at most 128 MiB of HBM per device.

```python
import jax
import jax.numpy as jnp
from jax import lax

D = 512
CLASSES = 1024
B_DEV = 32
M_DEV = 2048
BATCH = 4096
MEMORY = 262144
N_GRP = 8
N_DEV = 16


def labels_of(key, which, count):
    return jax.random.randint(jax.random.fold_in(key, which), (count,), 0, CLASSES)


def mixed_rows(key, which, labels, count):
    prototypes = jax.random.normal(jax.random.fold_in(key, 11), (CLASSES, D), jnp.float32)
    common = jax.random.normal(jax.random.fold_in(key, 12), (D,), jnp.float32)
    noise_rows = jax.random.normal(jax.random.fold_in(key, which), (count, D), jnp.float32)
    shared_part, class_part, noise_part = (0.67, 0.55, 0.5)
    values = shared_part * common[None, :] + class_part * prototypes[labels] + noise_part * noise_rows
    values = values / jnp.sqrt(1.0 * D)
    return jnp.clip(values, -30.0, 30.0)


def draw_batch_labels(key, part):
    return labels_of(key, 1, BATCH).astype(jnp.int32)


def draw_memory_labels(key, part):
    return labels_of(key, 2, MEMORY).astype(jnp.int32)


def draw_batch_rows(key, part):
    return mixed_rows(key, 3, labels_of(key, 1, BATCH), BATCH).astype(jnp.bfloat16)


def draw_memory(key, part):
    return mixed_rows(key, 4, labels_of(key, 2, MEMORY), MEMORY).astype(jnp.bfloat16)


def draw_keep_bits(key, part):
    tickets = jax.random.randint(jax.random.fold_in(key, 5), (MEMORY,), 0, 1000)
    position = jnp.arange(MEMORY).astype(jnp.int32)
    limits = 250 + 500 * position // MEMORY
    return (tickets < limits).astype(jnp.int32)


def setup_inputs(seed: int = 0) -> dict:
    seeds = jax.random.split(jax.random.key(seed), 7)
    return {
        "batch_rows": draw_batch_rows(jax.random.fold_in(seeds[6], 71), 0),
        "batch_labels": draw_batch_labels(jax.random.fold_in(seeds[6], 71), 0),
        "memory": draw_memory(jax.random.fold_in(seeds[6], 71), 0),
        "memory_labels": draw_memory_labels(jax.random.fold_in(seeds[6], 71), 0),
        "keep_bits": draw_keep_bits(jax.random.fold_in(seeds[6], 71), 0),
        "step_index": jax.random.randint(seeds[5], (1,), 0, 1000000).astype(jnp.int32),
    }


pos_scale = 2.0
neg_scale = 50.0
margin = 0.5

def normalize(values):
    floats = values.astype(jnp.float32)
    radius = jnp.sqrt(lax.optimization_barrier(jnp.sum(floats * floats, axis=1, keepdims=True)) + 1e-06)
    return (floats / radius, radius)

def reference(batch_rows, batch_labels, memory, memory_labels, keep_bits, step_index):
    unit_rows, radius = normalize(batch_rows)
    anchors = unit_rows.astype(jnp.bfloat16)
    memory_keys = normalize(memory)[0].astype(jnp.bfloat16)
    blocks = MEMORY // M_DEV
    key_blocks = memory_keys.reshape(blocks, M_DEV, D)
    label_blocks = memory_labels.reshape(blocks, M_DEV)
    kept_blocks = keep_bits.reshape(blocks, M_DEV)

    def visit(carry, inputs):
        pos_sum, neg_sum, pull, push = carry
        block_keys, block_labels, block_kept = inputs
        scores = lax.dot_general(anchors, block_keys, (((1,), (1,)), ((), ())), preferred_element_type=jnp.float32)
        same_class = batch_labels[:, None] == block_labels[None, :]
        kept_rows = (block_kept > 0)[None, :]
        positive = jnp.logical_and(same_class, kept_rows)
        negative = jnp.logical_and(jnp.logical_not(same_class), kept_rows)
        pos_term = jnp.where(positive, jnp.exp(-pos_scale * (scores - margin)), 0.0)
        neg_term = jnp.where(negative, jnp.exp(neg_scale * (scores - margin)), 0.0)
        pos_sum = pos_sum + lax.optimization_barrier(jnp.sum(pos_term, axis=1))
        neg_sum = neg_sum + lax.optimization_barrier(jnp.sum(neg_term, axis=1))
        pull = pull + jnp.dot(pos_term.astype(jnp.bfloat16), block_keys, preferred_element_type=jnp.float32)
        push = push + jnp.dot(neg_term.astype(jnp.bfloat16), block_keys, preferred_element_type=jnp.float32)
        return ((pos_sum, neg_sum, pull, push), None)
    zeros_row = jnp.zeros((BATCH,), jnp.float32)
    zeros_mat = jnp.zeros((BATCH, D), jnp.float32)
    (pos_sum, neg_sum, pull, push), _ = lax.scan(visit, (zeros_row, zeros_row, zeros_mat, zeros_mat), (key_blocks, label_blocks, kept_blocks))
    anchor_loss = jnp.log(1.0 + pos_sum) / pos_scale + jnp.log(1.0 + neg_sum) / neg_scale
    grad_unit = push / (1.0 + neg_sum)[:, None] - pull / (1.0 + pos_sum)[:, None]
    along = lax.optimization_barrier(jnp.sum(unit_rows * grad_unit, axis=1, keepdims=True))
    grad_batch = (grad_unit - unit_rows * along) / radius
    devices_all = N_GRP * N_DEV
    step_value = step_index[0]
    slot_index = (step_value % (M_DEV // B_DEV)).astype(jnp.int32)
    source = ((jnp.arange(devices_all).astype(jnp.int32) - step_value) % devices_all).astype(jnp.int32)
    moved_rows = anchors.reshape(devices_all, B_DEV, D)[source]
    moved_labels = batch_labels.reshape(devices_all, B_DEV)[source]
    zero_index = jnp.zeros((), jnp.int32)
    new_memory = lax.dynamic_update_slice(memory.reshape(devices_all, M_DEV, D), moved_rows, (zero_index, slot_index * B_DEV, zero_index))
    new_labels = lax.dynamic_update_slice(memory_labels.reshape(devices_all, M_DEV), moved_labels, (zero_index, slot_index * B_DEV))
    return (grad_batch, anchor_loss, new_memory.reshape(MEMORY, D), new_labels.reshape(MEMORY))
```

```python
import functools
import math

import jax
import jax.numpy as jnp
from jax import lax
from jax.experimental import pallas as pl
from jax.experimental.pallas import tpu as pltpu
from jax.sharding import PartitionSpec as P

F32, BF16, I32 = jnp.float32, jnp.bfloat16, jnp.int32
MESH = pl.DeviceIdType.MESH
LOG2E = math.log2(math.e)
EXP_NEG = math.exp(-25.0)
EXP_POS = math.exp(1.0)

ORDERS = ((0, 1, 2), (2, 0, 1))
STRIDES = (16, 4, 1)
ROWS = 16
CHUNK = 256
WIDTH = 512
KEYS_DEV = 2048
KEYS = 4096
S_TILE = 2048
VISIT = (0, 1, 3, 2)


def column(row):
    return jnp.transpose(jnp.broadcast_to(row, (128, 128)))


def unit_scale(values):
    return lax.rsqrt(jnp.sum(values * values, axis=1, keepdims=True) + 1e-06)


def kernel(
    step_ref, batch_ref, blab_ref, mlab_ref, keep_ref, mem_ref,
    grad_ref, loss_ref, moved_ref, mvlab_ref, newmem_ref,
    mraw, klraw, kpraw, keys, klab, raw, labs, an, labc, terms, acc, sums, sums_in, den,
    gpart, gown, sb1, rb1, g1, sb2, rb2, g2, sb3, rb3, cand, cand_in, clab, clab_in,
    mem_sem, out_sem, agd_s, agd_r, agl_s, agl_r, ar_s, ar_r, rs_s, rs_r, pt_s, pt_r, bt_s, bt_r,
):
    n_dev = lax.axis_size("dev")
    me = lax.axis_index("grp") * n_dev + lax.axis_index("dev")
    core = me % 2
    chip = me // 2
    at = (chip // 16, (chip // 4) % 4, chip % 4)

    def device(index):
        return (index // n_dev, index % n_dev)

    def peer(axis, off):
        there = (at[axis] + off) % 4
        return device(me + (there - at[axis]) * (2 * STRIDES[axis]))

    partner = device(me + 1 - 2 * core)

    def remote(src, dst, send, recv, to):
        return pltpu.make_async_remote_copy(
            src_ref=src, dst_ref=dst, send_sem=send, recv_sem=recv, device_id=to, device_id_type=MESH
        )

    own_mem = pltpu.make_async_copy(mem_ref, mraw.at[0], mem_sem)
    own_mem.start()

    barrier = pltpu.get_barrier_semaphore()
    for axis in range(3):
        for off in (1, 2, 3):
            pl.semaphore_signal(barrier, inc=1, device_id=peer(axis, off), device_id_type=MESH)
    pl.semaphore_signal(barrier, inc=1, device_id=partner, device_id_type=MESH)
    for p, (f, m, l) in enumerate(ORDERS):
        raw[p, at[l], at[m], at[f]] = batch_ref[pl.ds(p * ROWS, ROWS), :]
        labs[p, at[l], at[m], at[f]] = blab_ref[...]
    pl.semaphore_wait(barrier, 10)

    def slot(ref, p, phase, off):
        f, m, l = (at[a] for a in ORDERS[p])
        if phase == 0:
            return ref.at[p, l, m, (f + off) % 4]
        if phase == 1:
            return ref.at[p, l, (m + off) % 4]
        return ref.at[p, (l + off) % 4]

    def gather(p, phase, off, back):
        shift = 4 - off if back else 0
        to = peer(ORDERS[p][phase], off)
        rows, labels = slot(raw, p, phase, shift), slot(labs, p, phase, shift)
        return (
            remote(rows, rows, agd_s.at[p, phase, off - 1], agd_r.at[p, phase, off - 1], to),
            remote(labels, labels, agl_s.at[p, phase, off - 1], agl_r.at[p, phase, off - 1], to),
        )

    def gather_start(phase):
        for off in (1, 3, 2):
            for p in (0, 1):
                for copy in gather(p, phase, off, False):
                    copy.start()

    def gather_recv(phase):
        for p in (0, 1):
            for off in (1, 2, 3):
                for copy in gather(p, phase, off, True):
                    copy.wait_recv()

    gather_start(0)
    swaps = (
        remote(mem_ref, mraw.at[1], pt_s.at[0], pt_r.at[0], partner),
        remote(mlab_ref, klraw.at[1], pt_s.at[1], pt_r.at[1], partner),
        remote(keep_ref, kpraw.at[1], pt_s.at[2], pt_r.at[2], partner),
    )
    for copy in swaps:
        copy.start()

    klraw[0] = mlab_ref[...]
    kpraw[0] = keep_ref[...]

    def normalize_memory(half):
        def block(i, _):
            row = pl.multiple_of(i * 128, 128)
            kept = kpraw[half, :, pl.ds(row, 128)] > 0
            klab[half, :, pl.ds(row, 128)] = jnp.where(
                kept, klraw[half, :, pl.ds(row, 128)], -1
            ).astype(F32)
            values = mraw[half, pl.ds(row, 128), :].astype(F32)
            scale = unit_scale(values) * column(jnp.where(kept, 1.0, 0.0))[:, 0:1]
            keys[pl.ds(pl.multiple_of(half * KEYS_DEV + row, 128), 128), :] = (values * scale).astype(BF16)
            return 0

        lax.fori_loop(0, KEYS_DEV // 128, block, 0)

    own_mem.wait()
    out_mem = pltpu.make_async_copy(mraw.at[0], newmem_ref, out_sem)
    out_mem.start()
    normalize_memory(0)
    gather_recv(0)
    gather_start(1)
    for copy in swaps:
        copy.wait_recv()
    normalize_memory(1)
    gather_recv(1)
    gather_start(2)

    dropped = float(KEYS) - jnp.sum(
        jnp.where(kpraw[...] > 0, 1.0, 0.0).reshape(2, KEYS_DEV), axis=(0, 1), keepdims=True
    )

    def prepare(p, l):
        values = raw[p, l].reshape(CHUNK, WIDTH).astype(F32)
        an[p, l] = (values * unit_scale(values)).astype(BF16)
        pages = labs[p, l].reshape(16, 128).astype(F32)
        wide = jnp.transpose(jnp.concatenate([pages] * 8, axis=0))
        for b in range(16):
            labc[p, l, pl.ds(b * ROWS, ROWS), :] = jnp.broadcast_to(
                wide[p * ROWS : (p + 1) * ROWS, b : b + 1], (ROWS, 128)
            )

    def score(p, l):
        acc[...] = jnp.zeros_like(acc)

        def tile(t, _):
            first = pl.multiple_of(t * S_TILE, S_TILE)
            s = lax.dot_general(
                an[p, l], keys[pl.ds(first, S_TILE), :], (((1,), (1,)), ((), ())),
                preferred_element_type=F32,
            )
            labels = labc[p, l]
            all_sum, pos_sum = acc[0], acc[1]
            for j in range(S_TILE // 128):
                sj = s[:, j * 128 : (j + 1) * 128]
                same = labels == klab[t, :, j * 128 : (j + 1) * 128]
                e = jnp.exp2(sj * jnp.where(same, -2.0 * LOG2E, 50.0 * LOG2E))
                all_sum = all_sum + e
                pos_sum = pos_sum + jnp.where(same, e, 0.0)
                terms[p, l, :, pl.ds(pl.multiple_of(first + j * 128, 128), 128)] = e.astype(BF16)
            acc[0], acc[1] = all_sum, pos_sum
            return 0

        lax.fori_loop(0, KEYS // S_TILE, tile, 0)
        for h in (0, 1):
            half = pl.ds(h * 128, 128)
            total = jnp.sum(jnp.transpose(acc[0, half, :]), axis=0, keepdims=True)
            pos = jnp.sum(jnp.transpose(acc[1, half, :]), axis=0, keepdims=True)
            sums[0, p, l, h : h + 1, :] = total - pos - dropped
            sums[0, p, l, 2 + h : 3 + h, :] = pos

    def visit(i, _):
        off = jnp.where(i == 2, 3, jnp.where(i == 3, 2, i))
        for p in (0, 1):
            f, m, l = (at[a] for a in ORDERS[p])
            here = (l + 4 - off) % 4

            @pl.when(off > 0)
            def _():
                to = peer(ORDERS[p][2], 1)
                k = jnp.maximum(off - 1, 0)
                rows, labels = raw.at[p, here], labs.at[p, here]
                remote(rows, rows, agd_s.at[p, 2, k], agd_r.at[p, 2, k], to).wait_recv()
                remote(labels, labels, agl_s.at[p, 2, k], agl_r.at[p, 2, k], to).wait_recv()

            prepare(p, here)
            score(p, here)
        return 0

    lax.fori_loop(0, 4, visit, 0)

    for phase in range(3):
        copies = [
            remote(
                sums.at[phase], sums_in.at[phase, off - 1],
                ar_s.at[phase, off - 1], ar_r.at[phase, off - 1], peer(phase, off),
            )
            for off in (1, 2, 3)
        ]
        for copy in copies:
            copy.start()
        for copy in copies:
            copy.wait_recv()
        sums[phase + 1] = (
            sums[phase] + sums_in[phase, 0] + sums_in[phase, 1] + sums_in[phase, 2]
        )
        for copy in copies:
            copy.wait_send()

    def ring1(p, off):
        k = off - 1
        return remote(
            sb1.at[p, k], rb1.at[p, k], rs_s.at[p, 0, k], rs_r.at[p, 0, k], peer(ORDERS[p][2], off)
        )

    def grads(p, l):
        for h in (0, 1):
            half = pl.ds(h * 128, 128)
            den[p, l, 0, half, :] = column(1.0 + EXP_NEG * sums[3, p, l, h : h + 1, :])
            den[p, l, 1, half, :] = column(1.0 + EXP_POS * sums[3, p, l, 2 + h : 3 + h, :])
        gpart[...] = jnp.zeros_like(gpart)
        labels = labc[p, l]
        neg = EXP_NEG / den[p, l, 0]
        pos = -EXP_POS / den[p, l, 1]

        def tile(t, _):
            first = pl.multiple_of(t * S_TILE, S_TILE)
            parts = []
            for j in range(S_TILE // 128):
                e = terms[p, l, :, pl.ds(pl.multiple_of(first + j * 128, 128), 128)].astype(F32)
                same = labels == klab[t, :, j * 128 : (j + 1) * 128]
                parts.append((e * jnp.where(same, pos, neg)).astype(BF16))
            gpart[...] += jnp.dot(
                jnp.concatenate(parts, axis=1), keys[pl.ds(first, S_TILE), :],
                preferred_element_type=F32,
            )
            return 0

        lax.fori_loop(0, KEYS // S_TILE, tile, 0)

    def push(i, _):
        off = jnp.where(i == 0, 2, jnp.where(i == 1, 1, 3))
        for p in (0, 1):
            l = (at[ORDERS[p][2]] + off) % 4
            grads(p, l)
            sb1[p, off - 1] = gpart[...].astype(BF16)
            ring1(p, off).start()
        return 0

    lax.fori_loop(0, 3, push, 0)
    for p in (0, 1):
        grads(p, at[ORDERS[p][2]])
        gown[p] = gpart[...]

    step = step_ref[0]
    odd = step % 2
    mate = me + 1 - 2 * core
    asker = jnp.where(odd == 0, me, mate)
    block = ((asker + 1048576 - step) % 128) // 2
    wanted = jnp.full((ROWS, WIDTH), block, I32)
    wanted_row = jnp.full((1, 128), block, I32)

    def find(q, found):
        qx, qy, qz = q // 16, (q // 4) % 4, q % 4
        pick = wanted == q
        upper = an[0, qz, pl.ds(pl.multiple_of((qy * 4 + qx) * ROWS, ROWS), ROWS), :].astype(F32)
        lower = an[1, qy, pl.ds(pl.multiple_of((qx * 4 + qz) * ROWS, ROWS), ROWS), :].astype(F32)
        return (
            jnp.where(pick, upper, found[0]),
            jnp.where(pick, lower, found[1]),
            jnp.where(wanted_row == q, labs[0, qz, qy, qx], found[2]),
        )

    nothing = jnp.zeros((ROWS, WIDTH), F32)
    upper, lower, label_row = lax.fori_loop(
        0, 64, find, (nothing, nothing, jnp.zeros((1, 128), I32))
    )
    cand[pl.ds(0, ROWS), :] = upper.astype(BF16)
    cand[pl.ds(ROWS, ROWS), :] = lower.astype(BF16)
    clab[...] = label_row
    trade = (
        remote(cand, cand_in, bt_s.at[0], bt_r.at[0], partner),
        remote(clab, clab_in, bt_s.at[1], bt_r.at[1], partner),
    )
    for copy in trade:
        copy.start()

    def ring2(p, off):
        return remote(
            sb2.at[p, off - 1], rb2.at[p, off - 1], rs_s.at[p, 1, off - 1], rs_r.at[p, 1, off - 1],
            peer(ORDERS[p][1], off),
        )

    def ring3(p, off):
        return remote(
            sb3.at[p, off - 1], rb3.at[p, off - 1], rs_s.at[p, 2, off - 1], rs_r.at[p, 2, off - 1],
            peer(ORDERS[p][0], off),
        )

    for p in (0, 1):
        m = at[ORDERS[p][1]]
        for off in (1, 2, 3):
            ring1(p, off).wait_recv()
        g1[p] = (
            gown[p] + rb1[p, 0].astype(F32) + rb1[p, 1].astype(F32) + rb1[p, 2].astype(F32)
        ).reshape(4, 64, WIDTH)
        for off in (1, 2, 3):
            sb2[p, off - 1] = g1[p, (m + off) % 4].astype(BF16)
            ring2(p, off).start()
    for p in (0, 1):
        f, m = at[ORDERS[p][0]], at[ORDERS[p][1]]
        for off in (1, 2, 3):
            ring2(p, off).wait_recv()
        g2[p] = (
            g1[p, m] + rb2[p, 0].astype(F32) + rb2[p, 1].astype(F32) + rb2[p, 2].astype(F32)
        ).reshape(4, ROWS, WIDTH)
        for off in (1, 2, 3):
            sb3[p, off - 1] = g2[p, (f + off) % 4]
            ring3(p, off).start()
    for p in (0, 1):
        f, m, l = (at[a] for a in ORDERS[p])
        for off in (1, 2, 3):
            ring3(p, off).wait_recv()
        grad_unit = g2[p, f] + rb3[p, 0] + rb3[p, 1] + rb3[p, 2]
        values = batch_ref[pl.ds(p * ROWS, ROWS), :].astype(F32)
        radius = jnp.sqrt(jnp.sum(values * values, axis=1, keepdims=True) + 1e-06)
        unit = values / radius
        along = jnp.sum(unit * grad_unit, axis=1, keepdims=True)
        mine = pl.ds(p * ROWS, ROWS)
        grad_ref[mine, :] = (grad_unit - unit * along) / radius
        own = pl.ds(pl.multiple_of((m * 4 + f) * ROWS, ROWS), ROWS)
        loss_ref[mine, :] = jnp.log(den[p, l, 1, own, :]) / 2.0 + jnp.log(den[p, l, 0, own, :]) / 50.0

    for copy in trade:
        copy.wait_recv()
    keep_mine = jnp.full((2 * ROWS, WIDTH), odd, I32) == 0
    moved_ref[...] = jnp.where(keep_mine, cand[...].astype(F32), cand_in[...].astype(F32)).astype(BF16)
    mvlab_ref[...] = jnp.where(jnp.full((1, 128), odd, I32) == 0, clab[...], clab_in[...])

    out_mem.wait()
    for copy in swaps + trade:
        copy.wait_send()
    for p in (0, 1):
        for off in (1, 2, 3):
            for phase in range(3):
                for copy in gather(p, phase, off, False):
                    copy.wait_send()
            for ring in (ring1, ring2, ring3):
                ring(p, off).wait_send()


def per_device(batch_rows, batch_labels, memory, memory_labels, keep_bits, step_index):
    local_rows = batch_rows.shape[0]
    vmem = pl.BlockSpec(memory_space=pltpu.VMEM)
    dma = pltpu.SemaphoreType.DMA
    labels = jnp.pad(batch_labels, (0, 128 - local_rows)).reshape(1, 128)
    grad, loss, moved, moved_labels, kept_memory = pl.pallas_call(
        kernel,
        out_shape=(
            jax.ShapeDtypeStruct((local_rows, WIDTH), F32),
            jax.ShapeDtypeStruct((local_rows, 128), F32),
            jax.ShapeDtypeStruct((local_rows, WIDTH), BF16),
            jax.ShapeDtypeStruct((1, 128), I32),
            jax.ShapeDtypeStruct((KEYS_DEV, WIDTH), BF16),
        ),
        in_specs=[pl.BlockSpec(memory_space=pltpu.SMEM), vmem, vmem, vmem, vmem, pl.BlockSpec(memory_space=pl.ANY)],
        out_specs=(vmem, vmem, vmem, vmem, pl.BlockSpec(memory_space=pl.ANY)),
        scratch_shapes=[
            pltpu.VMEM((2, KEYS_DEV, WIDTH), BF16),
            pltpu.VMEM((2, 1, KEYS_DEV), I32),
            pltpu.VMEM((2, 1, KEYS_DEV), I32),
            pltpu.VMEM((KEYS, WIDTH), BF16),
            pltpu.VMEM((2, 1, KEYS_DEV), F32),
            pltpu.VMEM((2, 4, 4, 4, ROWS, WIDTH), BF16),
            pltpu.VMEM((2, 4, 4, 4, 1, 128), I32),
            pltpu.VMEM((2, 4, CHUNK, WIDTH), BF16),
            pltpu.VMEM((2, 4, CHUNK, 128), F32),
            pltpu.VMEM((2, 4, CHUNK, KEYS), BF16),
            pltpu.VMEM((2, CHUNK, 128), F32),
            pltpu.VMEM((4, 2, 4, 4, 128), F32),
            pltpu.VMEM((3, 3, 2, 4, 4, 128), F32),
            pltpu.VMEM((2, 4, 2, CHUNK, 128), F32),
            pltpu.VMEM((CHUNK, WIDTH), F32),
            pltpu.VMEM((2, CHUNK, WIDTH), F32),
            pltpu.VMEM((2, 3, CHUNK, WIDTH), BF16),
            pltpu.VMEM((2, 3, CHUNK, WIDTH), BF16),
            pltpu.VMEM((2, 4, 64, WIDTH), F32),
            pltpu.VMEM((2, 3, 64, WIDTH), BF16),
            pltpu.VMEM((2, 3, 64, WIDTH), BF16),
            pltpu.VMEM((2, 4, ROWS, WIDTH), F32),
            pltpu.VMEM((2, 3, ROWS, WIDTH), F32),
            pltpu.VMEM((2, 3, ROWS, WIDTH), F32),
            pltpu.VMEM((2 * ROWS, WIDTH), BF16),
            pltpu.VMEM((2 * ROWS, WIDTH), BF16),
            pltpu.VMEM((1, 128), I32),
            pltpu.VMEM((1, 128), I32),
            dma,
            dma,
            dma((2, 3, 3)), dma((2, 3, 3)), dma((2, 3, 3)), dma((2, 3, 3)),
            dma((3, 3)), dma((3, 3)),
            dma((2, 3, 3)), dma((2, 3, 3)),
            dma((3,)), dma((3,)), dma((2,)), dma((2,)),
        ],
        compiler_params=pltpu.CompilerParams(
            collective_id=0, has_side_effects=True, vmem_limit_bytes=60 * 1024 * 1024
        ),
        name="xbm",
    )(
        step_index,
        batch_rows,
        labels,
        memory_labels.reshape(1, KEYS_DEV),
        keep_bits.reshape(1, KEYS_DEV),
        memory,
    )
    slot = step_index[0] % (memory.shape[0] // local_rows)
    new_memory = lax.dynamic_update_slice_in_dim(kept_memory, moved, slot * local_rows, 0)
    new_labels = lax.dynamic_update_slice_in_dim(
        memory_labels, moved_labels[0, :local_rows], slot * local_rows, 0
    )
    return grad, loss[:, 0], new_memory, new_labels


def solution(mesh):
    rows = P(("grp", "dev"), None)
    flat = P(("grp", "dev"))
    return jax.shard_map(
        per_device,
        mesh=mesh,
        in_specs=(rows, flat, rows, flat, flat, P()),
        out_specs=(rows, flat, rows, flat),
        check_vma=False,
    )
```

```python
import functools
import math

import jax
import jax.numpy as jnp
from jax import lax
from jax.experimental import pallas as pl
from jax.experimental.pallas import tpu as pltpu
from jax.sharding import PartitionSpec as P

F32, BF16, I32 = jnp.float32, jnp.bfloat16, jnp.int32
MESH = pl.DeviceIdType.MESH
LOG2E = math.log2(math.e)
EXP_NEG = math.exp(-25.0)
EXP_POS = math.exp(1.0)

ORDERS = ((0, 1, 2), (2, 0, 1))
STRIDES = (16, 4, 1)
ROWS = 16
CHUNK = 256
WIDTH = 512
KEYS_DEV = 2048
KEYS = 4096
SLOTS = KEYS_DEV // (2 * ROWS)


def column(row):
    return jnp.transpose(jnp.broadcast_to(row, (128, 128)))


def unit_scale(values):
    return lax.rsqrt(jnp.sum(values * values, axis=1, keepdims=True) + 1e-06)


def kernel(
    step_ref, batch_ref, blab_ref, mlab_ref, keep_ref, mem_ref,
    grad_ref, loss_ref, moved_ref, mvlab_ref,
    mraw, klraw, kpraw, keys, klab, raw, labs, an, labc, terms, acc, sums, sums_in, den,
    pair, gown, sb1, rb1, g1, sb2, rb2, g2, sb3, rb3, cand, cand_in, clab, clab_in,
    mem_sem, agd_s, agd_r, agl_s, agl_r, ar_s, ar_r, rs_s, rs_r, pt_s, pt_r, bt_s, bt_r,
):
    n_dev = lax.axis_size("dev")
    me = lax.axis_index("grp") * n_dev + lax.axis_index("dev")
    core = me % 2
    chip = me // 2
    at = (chip // 16, (chip // 4) % 4, chip % 4)

    def device(index):
        return (index // n_dev, index % n_dev)

    def peer(axis, off):
        there = (at[axis] + off) % 4
        return device(me + (there - at[axis]) * (2 * STRIDES[axis]))

    partner = device(me + 1 - 2 * core)

    def remote(src, dst, send, recv, to):
        return pltpu.make_async_remote_copy(
            src_ref=src, dst_ref=dst, send_sem=send, recv_sem=recv, device_id=to, device_id_type=MESH
        )

    own_mem = pltpu.make_async_copy(mem_ref, mraw.at[0], mem_sem)
    own_mem.start()

    barrier = pltpu.get_barrier_semaphore()
    for axis in range(3):
        for off in (1, 2, 3):
            pl.semaphore_signal(barrier, inc=1, device_id=peer(axis, off), device_id_type=MESH)
    pl.semaphore_signal(barrier, inc=1, device_id=partner, device_id_type=MESH)
    for i in range(4):
        clab[:, 2 * ROWS * i : 2 * ROWS * (i + 1)] = blab_ref[...]
    for p, (f, m, l) in enumerate(ORDERS):
        raw[p, at[l], at[m], at[f]] = batch_ref[pl.ds(p * ROWS, ROWS), :]
        labs[p, at[l], at[m], at[f]] = clab[...]
    pl.semaphore_wait(barrier, 10)

    def slot(ref, p, phase, off):
        f, m, l = (at[a] for a in ORDERS[p])
        if phase == 0:
            return ref.at[p, l, m, (f + off) % 4]
        if phase == 1:
            return ref.at[p, l, (m + off) % 4]
        return ref.at[p, (l + off) % 4]

    def gather(p, phase, off, back):
        shift = 4 - off if back else 0
        to = peer(ORDERS[p][phase], off)
        rows, labels = slot(raw, p, phase, shift), slot(labs, p, phase, shift)
        return (
            remote(rows, rows, agd_s.at[p, phase, off - 1], agd_r.at[p, phase, off - 1], to),
            remote(labels, labels, agl_s.at[p, phase, off - 1], agl_r.at[p, phase, off - 1], to),
        )

    def gather_start(phase):
        for off in (1, 3, 2):
            for p in (0, 1):
                for copy in gather(p, phase, off, False):
                    copy.start()

    def gather_recv(phase):
        for p in (0, 1):
            for off in (1, 2, 3):
                for copy in gather(p, phase, off, True):
                    copy.wait_recv()

    gather_start(0)
    swaps = (
        remote(mem_ref, mraw.at[1], pt_s.at[0], pt_r.at[0], partner),
        remote(mlab_ref, klraw.at[1], pt_s.at[1], pt_r.at[1], partner),
        remote(keep_ref, kpraw.at[1], pt_s.at[2], pt_r.at[2], partner),
    )
    for copy in swaps:
        copy.start()

    klraw[0] = mlab_ref[...]
    kpraw[0] = keep_ref[...]

    def normalize_memory(half):
        def block(i, _):
            row = pl.multiple_of(i * 128, 128)
            kept = kpraw[half, :, pl.ds(row, 128)] > 0
            klab[:, pl.ds(pl.multiple_of(half * KEYS_DEV + row, 128), 128)] = jnp.where(
                kept, klraw[half, :, pl.ds(row, 128)], -1
            ).astype(F32)
            values = mraw[half, pl.ds(row, 128), :].astype(F32)
            scale = unit_scale(values) * column(jnp.where(kept, 1.0, 0.0))[:, 0:1]
            keys[pl.ds(pl.multiple_of(half * KEYS_DEV + row, 128), 128), :] = (values * scale).astype(BF16)
            return 0

        lax.fori_loop(0, KEYS_DEV // 128, block, 0)

    own_mem.wait()
    normalize_memory(0)
    gather_recv(0)
    gather_start(1)
    for copy in swaps:
        copy.wait_recv()
    normalize_memory(1)
    gather_recv(1)
    gather_start(2)

    dropped = float(KEYS) - jnp.sum(
        jnp.where(kpraw[...] > 0, 1.0, 0.0).reshape(2, KEYS_DEV), axis=(0, 1), keepdims=True
    )

    def prepare(p, l):
        values = raw[p, l].reshape(CHUNK, WIDTH).astype(F32)
        an[p, l] = (values * unit_scale(values)).astype(BF16)
        pages = labs[p, l].reshape(16, 128).astype(F32)
        wide = jnp.transpose(jnp.concatenate([pages] * 8, axis=0))
        mine = jnp.where(jnp.full((ROWS, 128), p, I32) == 0, wide[:ROWS], wide[ROWS : 2 * ROWS])
        for b in range(16):
            labc[p, l, pl.ds(b * ROWS, ROWS), :] = jnp.broadcast_to(mine[:, b : b + 1], (ROWS, 128))

    def score(p, l):
        s = lax.dot_general(
            an[p, l], keys[...], (((1,), (1,)), ((), ())), preferred_element_type=F32
        )
        labels = labc[p, l]
        all_sum = jnp.zeros((CHUNK, 128), F32)
        pos_sum = jnp.zeros((CHUNK, 128), F32)
        for j in range(0, KEYS, 128):
            same = labels == klab[:, j : j + 128]
            e = jnp.exp2(s[:, j : j + 128] * jnp.where(same, -2.0 * LOG2E, 50.0 * LOG2E))
            all_sum = all_sum + e
            pos_sum = pos_sum + jnp.where(same, e, 0.0)
            terms[p, l, :, j : j + 128] = e.astype(BF16)
        acc[0], acc[1] = all_sum, pos_sum
        for h in (0, 1):
            half = pl.ds(h * 128, 128)
            total = jnp.sum(jnp.transpose(acc[0, half, :]), axis=0, keepdims=True)
            pos = jnp.sum(jnp.transpose(acc[1, half, :]), axis=0, keepdims=True)
            sums[0, p, l, pl.ds(h, 1), :] = total - pos - dropped
            sums[0, p, l, pl.ds(2 + h, 1), :] = pos

    def last(p):
        return jnp.where(p == 0, at[2], at[1])

    def last_peer(p, off):
        there = (last(p) + off) % 4
        return device(me + (there - last(p)) * jnp.where(p == 0, 2 * STRIDES[2], 2 * STRIDES[1]))

    def visit(i, _):
        p, turn = i % 2, i // 2
        off = jnp.where(turn == 2, 3, jnp.where(turn == 3, 2, turn))
        here = (last(p) + 4 - off) % 4

        @pl.when(turn > 0)
        def _():
            k = jnp.maximum(off - 1, 0)
            rows, labels = raw.at[p, here], labs.at[p, here]
            remote(rows, rows, agd_s.at[p, 2, k], agd_r.at[p, 2, k], partner).wait_recv()
            remote(labels, labels, agl_s.at[p, 2, k], agl_r.at[p, 2, k], partner).wait_recv()

        prepare(p, here)
        score(p, here)
        return 0

    lax.fori_loop(0, 8, visit, 0)

    def part(p, l, weight):
        labels = labc[p, l]
        parts = []
        for j in range(0, KEYS, 128):
            same = labels == klab[:, j : j + 128]
            parts.append(weight(same, terms[p, l, :, j : j + 128].astype(F32)).astype(BF16))
        return jnp.dot(jnp.concatenate(parts, axis=1), keys[...], preferred_element_type=F32)

    def early(i):
        return i % 2, jnp.where(i == 2, 1, 2)

    def add_up(phase, _):
        coord = jnp.where(phase == 0, at[0], jnp.where(phase == 1, at[1], at[2]))
        stride = jnp.where(phase == 0, 2 * STRIDES[0], jnp.where(phase == 1, 2 * STRIDES[1], 2 * STRIDES[2]))
        copies = [
            remote(
                sums.at[phase], sums_in.at[phase, off - 1],
                ar_s.at[phase, off - 1], ar_r.at[phase, off - 1],
                device(me + ((coord + off) % 4 - coord) * stride),
            )
            for off in (1, 2, 3)
        ]
        for copy in copies:
            copy.start()
        p, off = early(phase)
        l = (last(p) + off) % 4
        pair[0, phase] = part(p, l, lambda same, e: jnp.where(same, 0.0, e))
        pair[1, phase] = part(p, l, lambda same, e: jnp.where(same, e, 0.0))
        for copy in copies:
            copy.wait_recv()
        sums[phase + 1] = (
            sums[phase] + sums_in[phase, 0] + sums_in[phase, 1] + sums_in[phase, 2]
        )
        for copy in copies:
            copy.wait_send()
        return 0

    lax.fori_loop(0, 3, add_up, 0)

    def ring1(p, off):
        k = jnp.maximum(off - 1, 0)
        return remote(
            sb1.at[p, k], rb1.at[p, k], rs_s.at[p, 0, k], rs_r.at[p, 0, k], last_peer(p, off)
        )

    def weights(p, l):
        for h in (0, 1):
            half = pl.ds(h * 128, 128)
            den[p, l, 0, half, :] = column(1.0 + EXP_NEG * sums[3, p, l, pl.ds(h, 1), :])
            den[p, l, 1, half, :] = column(1.0 + EXP_POS * sums[3, p, l, pl.ds(2 + h, 1), :])
        return EXP_NEG / den[p, l, 0], -EXP_POS / den[p, l, 1]

    def push_early(i, _):
        p, off = early(i)
        neg, pos = weights(p, (last(p) + off) % 4)
        for j in range(0, WIDTH, 128):
            some = pl.ds(j, 128)
            sb1[p, off - 1, :, some] = (
                pair[0, i, :, some] * neg + pair[1, i, :, some] * pos
            ).astype(BF16)
        ring1(p, off).start()
        return 0

    lax.fori_loop(0, 3, push_early, 0)

    def push(i, _):
        p, off = (i + 1) % 2, jnp.where(i == 0, 1, jnp.where(i < 3, 3, 0))
        l = (last(p) + off) % 4
        neg, pos = weights(p, l)
        g = part(p, l, lambda same, e: e * jnp.where(same, pos, neg))
        gown[p] = g

        @pl.when(i < 3)
        def _():
            sb1[p, jnp.maximum(off - 1, 0)] = g.astype(BF16)
            ring1(p, off).start()

        return 0

    lax.fori_loop(0, 5, push, 0)

    step = step_ref[0]
    odd = step % 2
    mate = me + 1 - 2 * core
    asker = jnp.where(odd == 0, me, mate)
    block = ((asker + 1048576 - step) % 128) // 2
    wanted = jnp.full((ROWS, WIDTH), block, I32)
    wanted_row = jnp.full((1, 128), block, I32)

    def find(q, found):
        qx, qy, qz = q // 16, (q // 4) % 4, q % 4
        pick = wanted == q
        upper = an[0, qz, pl.ds(pl.multiple_of((qy * 4 + qx) * ROWS, ROWS), ROWS), :].astype(F32)
        lower = an[1, qy, pl.ds(pl.multiple_of((qx * 4 + qz) * ROWS, ROWS), ROWS), :].astype(F32)
        return (
            jnp.where(pick, upper, found[0]),
            jnp.where(pick, lower, found[1]),
            jnp.where(wanted_row == q, labs[0, qz, qy, qx], found[2]),
        )

    nothing = jnp.zeros((ROWS, WIDTH), F32)
    upper, lower, label_row = lax.fori_loop(
        0, 64, find, (nothing, nothing, jnp.zeros((1, 128), I32))
    )
    cand[pl.ds(0, ROWS), :] = upper.astype(BF16)
    cand[pl.ds(ROWS, ROWS), :] = lower.astype(BF16)
    clab[...] = label_row
    trade = (
        remote(cand, cand_in, bt_s.at[0], bt_r.at[0], partner),
        remote(clab, clab_in, bt_s.at[1], bt_r.at[1], partner),
    )
    for copy in trade:
        copy.start()

    def ring2(p, off):
        return remote(
            sb2.at[p, off - 1], rb2.at[p, off - 1], rs_s.at[p, 1, off - 1], rs_r.at[p, 1, off - 1],
            peer(ORDERS[p][1], off),
        )

    def ring3(p, off):
        return remote(
            sb3.at[p, off - 1], rb3.at[p, off - 1], rs_s.at[p, 2, off - 1], rs_r.at[p, 2, off - 1],
            peer(ORDERS[p][0], off),
        )

    for p in (0, 1):
        m = at[ORDERS[p][1]]
        for off in (1, 2, 3):
            ring1(p, off).wait_recv()
        g1[p] = (
            gown[p] + rb1[p, 0].astype(F32) + rb1[p, 1].astype(F32) + rb1[p, 2].astype(F32)
        ).reshape(4, 64, WIDTH)
        for off in (1, 2, 3):
            sb2[p, off - 1] = g1[p, (m + off) % 4].astype(BF16)
            ring2(p, off).start()
    for p in (0, 1):
        f, m = at[ORDERS[p][0]], at[ORDERS[p][1]]
        for off in (1, 2, 3):
            ring2(p, off).wait_recv()
        g2[p] = (
            g1[p, m] + rb2[p, 0].astype(F32) + rb2[p, 1].astype(F32) + rb2[p, 2].astype(F32)
        ).reshape(4, ROWS, WIDTH)
        for off in (1, 2, 3):
            sb3[p, off - 1] = g2[p, (f + off) % 4]
            ring3(p, off).start()
    for p in (0, 1):
        f, m, l = (at[a] for a in ORDERS[p])
        for off in (1, 2, 3):
            ring3(p, off).wait_recv()
        grad_unit = g2[p, f] + rb3[p, 0] + rb3[p, 1] + rb3[p, 2]
        values = batch_ref[pl.ds(p * ROWS, ROWS), :].astype(F32)
        radius = jnp.sqrt(jnp.sum(values * values, axis=1, keepdims=True) + 1e-06)
        unit = values / radius
        along = jnp.sum(unit * grad_unit, axis=1, keepdims=True)
        mine = pl.ds(p * ROWS, ROWS)
        grad_ref[mine, :] = (grad_unit - unit * along) / radius
        own = pl.ds(pl.multiple_of((m * 4 + f) * ROWS, ROWS), ROWS)
        loss_ref[mine, :] = jnp.log(den[p, l, 1, own, :]) / 2.0 + jnp.log(den[p, l, 0, own, :]) / 50.0

    for copy in trade:
        copy.wait_recv()
    keep_mine = jnp.full((2 * ROWS, WIDTH), odd, I32) == 0
    moved_ref[...] = jnp.where(keep_mine, cand[...].astype(F32), cand_in[...].astype(F32)).astype(BF16)
    mvlab_ref[...] = jnp.where(jnp.full((1, 128), odd, I32) == 0, clab[...], clab_in[...])

    for copy in swaps + trade:
        copy.wait_send()
    for p in (0, 1):
        for off in (1, 2, 3):
            for phase in range(3):
                for copy in gather(p, phase, off, False):
                    copy.wait_send()
            for ring in (ring1, ring2, ring3):
                ring(p, off).wait_send()


def finish(
    step_ref, grad_ref, loss_ref, moved_ref, mvlab_ref, mlab_ref, mem_ref,
    grad_out, loss_out, lab_out, mem_out, buf, sem_in, sem_out,
):
    pieces, size = buf.shape[0], buf.shape[1]
    slot = step_ref[0] % SLOTS
    loads = [
        pltpu.make_async_copy(mem_ref.at[pl.ds(i * size, size)], buf.at[i], sem_in.at[i])
        for i in range(pieces)
    ]
    stores = [
        pltpu.make_async_copy(buf.at[i], mem_out.at[pl.ds(i * size, size)], sem_out.at[i])
        for i in range(pieces)
    ]
    for load in loads:
        load.start()
    grad_out[...] = grad_ref[...]
    rows = loss_ref.shape[0]
    diagonal = lax.broadcasted_iota(I32, (rows, 128), 0) == lax.broadcasted_iota(I32, (rows, 128), 1)
    loss_out[...] = jnp.sum(jnp.where(diagonal, loss_ref[...], 0.0), axis=0, keepdims=True)[:, :rows]
    lane = lax.broadcasted_iota(I32, (1, 128), 1) // (2 * ROWS)
    for i in range(KEYS_DEV // 128):
        here = pl.ds(i * 128, 128)
        lab_out[:, here] = jnp.where(
            lane + i * (64 // ROWS) == jnp.full((1, 128), slot, I32), mvlab_ref[...], mlab_ref[:, here]
        )
    per_piece = size // (2 * ROWS)
    for i in range(pieces):
        loads[i].wait()

        @pl.when(slot // per_piece == i)
        def _():
            at = pl.multiple_of((slot % per_piece) * (2 * ROWS), 2 * ROWS)
            buf[i, pl.ds(at, 2 * ROWS), :] = moved_ref[...]

        stores[i].start()
    for store in stores:
        store.wait()


def per_device(batch_rows, batch_labels, memory, memory_labels, keep_bits, step_index):
    local_rows = batch_rows.shape[0]
    vmem = pl.BlockSpec(memory_space=pltpu.VMEM)
    dma = pltpu.SemaphoreType.DMA
    memory_labels_row = memory_labels.reshape(1, KEYS_DEV)
    grad, loss, moved, moved_labels = pl.pallas_call(
        kernel,
        out_shape=(
            jax.ShapeDtypeStruct((local_rows, WIDTH), F32),
            jax.ShapeDtypeStruct((local_rows, 128), F32),
            jax.ShapeDtypeStruct((local_rows, WIDTH), BF16),
            jax.ShapeDtypeStruct((1, 128), I32),
        ),
        in_specs=[pl.BlockSpec(memory_space=pltpu.SMEM), vmem, vmem, vmem, vmem, pl.BlockSpec(memory_space=pl.ANY)],
        out_specs=(vmem, vmem, vmem, vmem),
        scratch_shapes=[
            pltpu.VMEM((2, KEYS_DEV, WIDTH), BF16),
            pltpu.VMEM((2, 1, KEYS_DEV), I32),
            pltpu.VMEM((2, 1, KEYS_DEV), I32),
            pltpu.VMEM((KEYS, WIDTH), BF16),
            pltpu.VMEM((1, KEYS), F32),
            pltpu.VMEM((2, 4, 4, 4, ROWS, WIDTH), BF16),
            pltpu.VMEM((2, 4, 4, 4, 1, 128), I32),
            pltpu.VMEM((2, 4, CHUNK, WIDTH), BF16),
            pltpu.VMEM((2, 4, CHUNK, 128), F32),
            pltpu.VMEM((2, 4, CHUNK, KEYS), BF16),
            pltpu.VMEM((2, CHUNK, 128), F32),
            pltpu.VMEM((4, 2, 4, 4, 128), F32),
            pltpu.VMEM((3, 3, 2, 4, 4, 128), F32),
            pltpu.VMEM((2, 4, 2, CHUNK, 128), F32),
            pltpu.VMEM((2, 3, CHUNK, WIDTH), F32),
            pltpu.VMEM((2, CHUNK, WIDTH), F32),
            pltpu.VMEM((2, 3, CHUNK, WIDTH), BF16),
            pltpu.VMEM((2, 3, CHUNK, WIDTH), BF16),
            pltpu.VMEM((2, 4, 64, WIDTH), F32),
            pltpu.VMEM((2, 3, 64, WIDTH), BF16),
            pltpu.VMEM((2, 3, 64, WIDTH), BF16),
            pltpu.VMEM((2, 4, ROWS, WIDTH), F32),
            pltpu.VMEM((2, 3, ROWS, WIDTH), F32),
            pltpu.VMEM((2, 3, ROWS, WIDTH), F32),
            pltpu.VMEM((2 * ROWS, WIDTH), BF16),
            pltpu.VMEM((2 * ROWS, WIDTH), BF16),
            pltpu.VMEM((1, 128), I32),
            pltpu.VMEM((1, 128), I32),
            dma,
            dma((2, 3, 3)), dma((2, 3, 3)), dma((2, 3, 3)), dma((2, 3, 3)),
            dma((3, 3)), dma((3, 3)),
            dma((2, 3, 3)), dma((2, 3, 3)),
            dma((3,)), dma((3,)), dma((2,)), dma((2,)),
        ],
        compiler_params=pltpu.CompilerParams(
            collective_id=0, has_side_effects=True, vmem_limit_bytes=60 * 1024 * 1024
        ),
        name="xbm",
    )(
        step_index,
        batch_rows,
        batch_labels.reshape(1, local_rows),
        memory_labels_row,
        keep_bits.reshape(1, KEYS_DEV),
        memory,
    )
    smem, hbm = pl.BlockSpec(memory_space=pltpu.SMEM), pl.BlockSpec(memory_space=pl.ANY)
    pieces = 4
    grad, loss_row, new_labels, new_memory = pl.pallas_call(
        finish,
        out_shape=(
            jax.ShapeDtypeStruct((local_rows, WIDTH), F32),
            jax.ShapeDtypeStruct((1, local_rows), F32),
            jax.ShapeDtypeStruct((1, KEYS_DEV), I32),
            jax.ShapeDtypeStruct((KEYS_DEV, WIDTH), BF16),
        ),
        in_specs=[smem, vmem, vmem, vmem, vmem, vmem, hbm],
        out_specs=(vmem, vmem, vmem, hbm),
        scratch_shapes=[
            pltpu.VMEM((pieces, KEYS_DEV // pieces, WIDTH), BF16), dma((pieces,)), dma((pieces,)),
        ],
        name="finish",
    )(step_index, grad, loss, moved, moved_labels, memory_labels_row, memory)
    return grad, loss_row.reshape(local_rows), new_memory, new_labels.reshape(KEYS_DEV)


def solution(mesh):
    rows = P(("grp", "dev"), None)
    flat = P(("grp", "dev"))
    return jax.shard_map(
        per_device,
        mesh=mesh,
        in_specs=(rows, flat, rows, flat, flat, P()),
        out_specs=(rows, flat, rows, flat),
        check_vma=False,
    )
```

```python
import functools
import math

import jax
import jax.numpy as jnp
from jax import lax
from jax.experimental import pallas as pl
from jax.experimental.pallas import tpu as pltpu
from jax.sharding import PartitionSpec as P

F32, BF16, I32 = jnp.float32, jnp.bfloat16, jnp.int32
MESH = pl.DeviceIdType.MESH
LOG2E = math.log2(math.e)
EXP_NEG = math.exp(-25.0)
EXP_POS = math.exp(1.0)

ROWS = 16
CHUNK = 256
WIDTH = 512
KEYS_DEV = 2048
KEYS = 4096
SLOTS = KEYS_DEV // (2 * ROWS)


def column(row):
    return jnp.transpose(jnp.broadcast_to(row, (128, 128)))


def unit_scale(values):
    return lax.rsqrt(jnp.sum(values * values, axis=1, keepdims=True) + 1e-06)


def kernel(
    step_ref, batch_ref, blab_ref, mlab_ref, keep_ref, mem_ref,
    grad_ref, loss_ref, moved_ref, mvlab_ref,
    mraw, klraw, kpraw, keys, klab, raw, labs, an, labc, terms, acc, sums, sums_in, sums_z, den,
    pair, gown, sb1, rb1, hb, gr, g1, sb2, rb2, cand, cand_in, clab, clab_in,
    mem_sem, pl_s, pl_r, pll_s, pll_r, ln_s, ln_r, lnl_s, lnl_r, fw_s, fw_r,
    as_s, as_r, az_s, az_r, h1_s, h1_r, r1_s, r1_r, r2_s, r2_r, pt_s, pt_r, bt_s, bt_r,
):
    n_dev = lax.axis_size("dev")
    me = lax.axis_index("grp") * n_dev + lax.axis_index("dev")
    core = me % 2
    chip = me // 2
    at = (chip // 16, (chip // 4) % 4, chip % 4)

    def device(index):
        return (index // n_dev, index % n_dev)

    def chip_at(dx, dy, dz):
        there = ((at[0] + dx) % 4) * 16 + ((at[1] + dy) % 4) * 4 + (at[2] + dz) % 4
        return device(2 * there + core)

    def peer(p, dl, dm, df):
        first, even = p == 0, core == 0
        dx = jnp.where(first, df, jnp.where(even, dm, dl))
        dy = jnp.where(first, dm, jnp.where(even, dl, dm))
        dz = jnp.where(first, dl, df)
        return chip_at(dx, dy, dz)

    def place(p):
        first, even = p == 0, core == 0
        last = jnp.where(first, at[2], jnp.where(even, at[1], at[0]))
        middle = jnp.where(first, at[1], jnp.where(even, at[0], at[1]))
        return last, middle, jnp.where(first, at[0], at[2])

    partner = device(me + 1 - 2 * core)

    def remote(src, dst, send, recv, to):
        return pltpu.make_async_remote_copy(
            src_ref=src, dst_ref=dst, send_sem=send, recv_sem=recv, device_id=to, device_id_type=MESH
        )

    own_mem = pltpu.make_async_copy(mem_ref, mraw.at[0], mem_sem)
    own_mem.start()

    barrier = pltpu.get_barrier_semaphore()
    def greet(p, dl, dm, df):
        pl.semaphore_signal(barrier, inc=1, device_id=peer(p, dl, dm, df), device_id_type=MESH)

    def greet_plane(j, _):
        greet(0, 0, j // 4, j % 4)
        return 0

    def greet_diagonal(j, _):
        greet(1, 0, 1 + j // 3, 1 + j % 3)
        return 0

    lax.fori_loop(1, 16, greet_plane, 0)
    lax.fori_loop(0, 9, greet_diagonal, 0)
    for off in (1, 2, 3):
        greet(0, off, 0, 0)
    pl.semaphore_signal(barrier, inc=1, device_id=partner, device_id_type=MESH)
    for i in range(4):
        clab[:, 2 * ROWS * i : 2 * ROWS * (i + 1)] = blab_ref[...]
    for p in (0, 1):
        l, m, f = place(p)
        raw[p, l, m, f] = batch_ref[pl.ds(p * ROWS, ROWS), :]
        labs[p, l, m, f] = clab[...]
    pl.semaphore_wait(barrier, 28)

    def to_plane(p, j, back):
        l, m, f = place(p)
        dm, df = j // 4, j % 4
        if back:
            m, f = (m + 4 - dm) % 4, (f + 4 - df) % 4
        rows, labels, to = raw.at[p, l, m, f], labs.at[p, l, m, f], peer(p, 0, dm, df)
        return (
            remote(rows, rows, pl_s.at[p, j - 1], pl_r.at[p, j - 1], to),
            remote(labels, labels, pll_s.at[p, j - 1], pll_r.at[p, j - 1], to),
        )

    def plane_start(j, _):
        for p in (0, 1):
            for copy in to_plane(p, j, False):
                copy.start()
        return 0

    def plane_recv(j, _):
        for p in (0, 1):
            for copy in to_plane(p, j, True):
                copy.wait_recv()
        return 0

    def plane_sent(j, _):
        for p in (0, 1):
            for copy in to_plane(p, j, False):
                copy.wait_send()
        return 0

    def line_rows(p, off, back):
        l = place(p)[0]
        if back:
            l = (l + 4 - off) % 4
        rows = raw.at[p, l]
        return remote(rows, rows, ln_s.at[p, off // 2], ln_r.at[p, off // 2], peer(p, off, 0, 0))

    def line_labels(p, off, back):
        l = place(p)[0]
        if back:
            l = (l + 4 - off) % 4
        labels = labs.at[p, l]
        return remote(labels, labels, lnl_s.at[p, off - 1], lnl_r.at[p, off - 1], peer(p, off, 0, 0))

    def relay(p, off, back):
        l = place(p)[0]
        l = (l + (2 if back else 4 - off)) % 4
        half = raw.at[p, l, pl.ds(0 if off == 1 else 2, 2)]
        return remote(half, half, fw_s.at[p, off // 2], fw_r.at[p, off // 2], peer(p, off, 0, 0))

    lax.fori_loop(1, 16, plane_start, 0)
    swaps = (
        remote(mem_ref, mraw.at[1], pt_s.at[0], pt_r.at[0], partner),
        remote(mlab_ref, klraw.at[1], pt_s.at[1], pt_r.at[1], partner),
        remote(keep_ref, kpraw.at[1], pt_s.at[2], pt_r.at[2], partner),
    )
    for copy in swaps:
        copy.start()

    klraw[0] = mlab_ref[...]
    kpraw[0] = keep_ref[...]

    def normalize_memory(half):
        def block(i, _):
            row = pl.multiple_of(i * 128, 128)
            kept = kpraw[half, :, pl.ds(row, 128)] > 0
            klab[:, pl.ds(pl.multiple_of(half * KEYS_DEV + row, 128), 128)] = jnp.where(
                kept, klraw[half, :, pl.ds(row, 128)], -1
            ).astype(F32)
            values = mraw[half, pl.ds(row, 128), :].astype(F32)
            scale = unit_scale(values) * column(jnp.where(kept, 1.0, 0.0))[:, 0:1]
            keys[pl.ds(pl.multiple_of(half * KEYS_DEV + row, 128), 128), :] = (values * scale).astype(BF16)
            return 0

        lax.fori_loop(0, KEYS_DEV // 128, block, 0)

    own_mem.wait()
    normalize_memory(0)
    lax.fori_loop(1, 16, plane_recv, 0)
    for p in (1, 0):
        for off in (1, 3):
            line_rows(p, off, False).start()
        for off in (1, 3, 2):
            line_labels(p, off, False).start()
    for copy in swaps:
        copy.wait_recv()
    normalize_memory(1)

    dropped = float(KEYS) - jnp.sum(
        jnp.where(kpraw[...] > 0, 1.0, 0.0).reshape(2, KEYS_DEV), axis=(0, 1), keepdims=True
    )

    def prepare(p, l):
        values = raw[p, l].reshape(CHUNK, WIDTH).astype(F32)
        an[p, l] = (values * unit_scale(values)).astype(BF16)
        pages = labs[p, l].reshape(16, 128).astype(F32)
        wide = jnp.transpose(jnp.concatenate([pages] * 8, axis=0))
        mine = jnp.where(jnp.full((ROWS, 128), p, I32) == 0, wide[:ROWS], wide[ROWS : 2 * ROWS])
        for b in range(16):
            labc[p, l, pl.ds(b * ROWS, ROWS), :] = jnp.broadcast_to(mine[:, b : b + 1], (ROWS, 128))

    def score(p, l):
        s = lax.dot_general(
            an[p, l], keys[...], (((1,), (1,)), ((), ())), preferred_element_type=F32
        )
        labels = labc[p, l]
        all_sum = jnp.zeros((CHUNK, 128), F32)
        pos_sum = jnp.zeros((CHUNK, 128), F32)
        for j in range(0, KEYS, 128):
            same = labels == klab[:, j : j + 128]
            e = jnp.exp2(s[:, j : j + 128] * jnp.where(same, -2.0 * LOG2E, 50.0 * LOG2E))
            all_sum = all_sum + e
            pos_sum = pos_sum + jnp.where(same, e, 0.0)
            terms[p, l, :, j : j + 128] = e.astype(BF16)
        acc[0], acc[1] = all_sum, pos_sum
        for h in (0, 1):
            half = pl.ds(h * 128, 128)
            total = jnp.sum(jnp.transpose(acc[0, half, :]), axis=0, keepdims=True)
            pos = jnp.sum(jnp.transpose(acc[1, half, :]), axis=0, keepdims=True)
            sums[0, p, l, pl.ds(h, 1), :] = total - pos - dropped
            sums[0, p, l, pl.ds(2 + h, 1), :] = pos

    def visit(i, _):
        early_piece = jnp.logical_or(jnp.logical_or(i == 1, i == 2), jnp.logical_or(i == 3, i == 6))
        p = jnp.where(early_piece, 1, 0)
        off = jnp.where(i < 2, 0, jnp.where(i > 5, 2, jnp.where(i % 2 == 0, 1, 3)))
        here = (place(p)[0] + 4 - off) % 4

        @pl.when(jnp.logical_or(i == 2, i == 4))
        def _():
            for off in (1, 3):
                line_rows(p, off, True).wait_recv()
                relay(p, off, False).start()
                line_labels(p, off, True).wait_recv()

        @pl.when(i > 5)
        def _():
            for off in (1, 3):
                relay(p, off, True).wait_recv()
            line_labels(p, 2, True).wait_recv()

        prepare(p, here)
        score(p, here)
        return 0

    lax.fori_loop(0, 8, visit, 0)

    def part(p, l, weight):
        labels = labc[p, l]
        parts = []
        for j in range(0, KEYS, 128):
            same = labels == klab[:, j : j + 128]
            parts.append(weight(same, terms[p, l, :, j : j + 128].astype(F32)).astype(BF16))
        return jnp.dot(jnp.concatenate(parts, axis=1), keys[...], preferred_element_type=F32)

    def early(i):
        return i % 2, jnp.where(i == 2, 1, 2)

    def alone(i):
        p, off = early(i)
        l = (place(p)[0] + off) % 4
        pair[0, i] = part(p, l, lambda same, e: jnp.where(same, 0.0, e))
        pair[1, i] = part(p, l, lambda same, e: jnp.where(same, e, 0.0))

    def sums_plane(j):
        return remote(
            sums.at[0], sums_in.at[j - 1], as_s.at[j - 1], as_r.at[j - 1], chip_at(j % 4, j // 4, 0)
        )

    def sums_line(off):
        return remote(
            sums.at[1], sums_z.at[off - 1], az_s.at[off - 1], az_r.at[off - 1], chip_at(0, 0, off)
        )

    def add_up(i, _):
        @pl.when(i == 0)
        def _():
            def begin(j, _):
                sums_plane(j).start()
                return 0

            lax.fori_loop(1, 16, begin, 0)

        alone(i)

        @pl.when(i == 1)
        def _():
            def arrive(j, _):
                sums_plane(j).wait_recv()
                return 0

            lax.fori_loop(1, 16, arrive, 0)
            total = sums[0]
            for j in range(15):
                total = total + sums_in[j]
            sums[1] = total
            for off in (1, 3, 2):
                sums_line(off).start()

        return 0

    lax.fori_loop(0, 3, add_up, 0)
    for off in (1, 2, 3):
        sums_line(off).wait_recv()
    sums[2] = sums[1] + sums_z[0] + sums_z[1] + sums_z[2]

    def onward(p, off):
        side = off // 2
        return remote(
            sb1.at[p, 2, side], hb.at[p, side], h1_s.at[p, side], h1_r.at[p, side], peer(p, off, 0, 0)
        )

    def ring1(p, off, half):
        side = off // 2
        return remote(
            sb1.at[p, side, half], rb1.at[p, side, half],
            r1_s.at[p, side, half], r1_r.at[p, side, half], peer(p, off, 0, 0),
        )

    def dispatch(p, off, g):
        side = off // 2
        gr[p, side] = jnp.where(jnp.full((128, WIDTH), side, I32) == 0, g[:128], g[128:])
        sb1[p, side, 1 - side] = jnp.where(
            jnp.full((128, WIDTH), side, I32) == 0, g[128:], g[:128]
        ).astype(BF16)
        ring1(p, off, 1 - side).start()

    def complete(p, off):
        side = off // 2
        onward(p, off).wait_recv()
        sb1[p, side, side] = (gr[p, side] + hb[p, side].astype(F32)).astype(BF16)
        ring1(p, off, side).start()

    def weights(p, l):
        for h in (0, 1):
            half = pl.ds(h * 128, 128)
            den[p, l, 0, half, :] = column(1.0 + EXP_NEG * sums[2, p, l, pl.ds(h, 1), :])
            den[p, l, 1, half, :] = column(1.0 + EXP_POS * sums[2, p, l, pl.ds(2 + h, 1), :])
        return EXP_NEG / den[p, l, 0], -EXP_POS / den[p, l, 1]

    def ready(i):
        p, off = early(i)
        neg, pos = weights(p, (place(p)[0] + off) % 4)
        return jnp.concatenate(
            [
                pair[0, i, :, j : j + 128] * neg + pair[1, i, :, j : j + 128] * pos
                for j in range(0, WIDTH, 128)
            ],
            axis=1,
        )

    def push_early(p, _):
        sb1[p, 2] = ready(p).astype(BF16).reshape(2, 128, WIDTH)
        for off in (1, 3):
            onward(p, off).start()
        return 0

    lax.fori_loop(0, 2, push_early, 0)
    dispatch(0, 1, ready(2))

    def push(i, _):
        p, off = (i + 1) % 2, jnp.where(i == 0, 1, jnp.where(i < 3, 3, 0))
        l = (place(p)[0] + off) % 4
        neg, pos = weights(p, l)
        gown[p] = part(p, l, lambda same, e: e * jnp.where(same, pos, neg))

        @pl.when(i == 0)
        def _():
            dispatch(1, 1, gown[1])

        @pl.when(i == 1)
        def _():
            dispatch(0, 3, gown[0])
            complete(1, 1)

        @pl.when(i == 2)
        def _():
            dispatch(1, 3, gown[1])
            complete(0, 1)
            complete(0, 3)
            complete(1, 3)

        return 0

    lax.fori_loop(0, 5, push, 0)

    def ring2(p, j):
        l, m, f = place(p)
        dm, df = j // 4, j % 4
        block = ((m + dm) % 4) * 4 + (f + df) % 4
        return remote(
            sb2.at[p, block], rb2.at[p, j - 1], r2_s.at[p, j - 1], r2_r.at[p, j - 1], peer(p, 0, dm, df)
        )

    for p in (0, 1):
        for off in (1, 3):
            for half in (0, 1):
                ring1(p, off, half).wait_recv()
        g1[p] = (
            gown[p].reshape(2, 128, WIDTH) + rb1[p, 0].astype(F32) + rb1[p, 1].astype(F32)
        ).reshape(16, ROWS, WIDTH)
        sb2[p] = g1[p].astype(BF16)

        def begin(j, _):
            ring2(p, j).start()
            return 0

        lax.fori_loop(1, 16, begin, 0)

    step = step_ref[0]
    odd = step % 2
    mate = me + 1 - 2 * core
    asker = jnp.where(odd == 0, me, mate)
    block = ((asker + 1048576 - step) % 128) // 2
    wanted = jnp.full((ROWS, WIDTH), block, I32)
    wanted_row = jnp.full((1, 128), block, I32)

    def find(q, found):
        qx, qy, qz = q // 16, (q // 4) % 4, q % 4
        pick = wanted == q
        upper = an[0, qz, pl.ds(pl.multiple_of((qy * 4 + qx) * ROWS, ROWS), ROWS), :].astype(F32)
        ql, qm = jnp.where(core == 0, qy, qx), jnp.where(core == 0, qx, qy)
        lower = an[1, ql, pl.ds(pl.multiple_of((qm * 4 + qz) * ROWS, ROWS), ROWS), :].astype(F32)
        return (
            jnp.where(pick, upper, found[0]),
            jnp.where(pick, lower, found[1]),
            jnp.where(wanted_row == q, labs[0, qz, qy, qx], found[2]),
        )

    nothing = jnp.zeros((ROWS, WIDTH), F32)
    upper, lower, label_row = lax.fori_loop(
        0, 64, find, (nothing, nothing, jnp.zeros((1, 128), I32))
    )
    cand[pl.ds(0, ROWS), :] = upper.astype(BF16)
    cand[pl.ds(ROWS, ROWS), :] = lower.astype(BF16)
    clab[...] = label_row
    trade = (
        remote(cand, cand_in, bt_s.at[0], bt_r.at[0], partner),
        remote(clab, clab_in, bt_s.at[1], bt_r.at[1], partner),
    )
    for copy in trade:
        copy.start()

    for p in (0, 1):
        l, m, f = place(p)
        own = pl.ds(pl.multiple_of((m * 4 + f) * ROWS, ROWS), ROWS)
        mine = pl.ds(p * ROWS, ROWS)
        loss_ref[mine, :] = jnp.log(den[p, l, 1, own, :]) / 2.0 + jnp.log(den[p, l, 0, own, :]) / 50.0
    for p in (0, 1):
        l, m, f = place(p)

        def arrive(j, _):
            ring2(p, j).wait_recv()
            return 0

        lax.fori_loop(1, 16, arrive, 0)
        grad_unit = g1[p, m * 4 + f]
        for j in range(15):
            grad_unit = grad_unit + rb2[p, j].astype(F32)
        values = batch_ref[pl.ds(p * ROWS, ROWS), :].astype(F32)
        radius = jnp.sqrt(jnp.sum(values * values, axis=1, keepdims=True) + 1e-06)
        unit = values / radius
        along = jnp.sum(unit * grad_unit, axis=1, keepdims=True)
        grad_ref[pl.ds(p * ROWS, ROWS), :] = (grad_unit - unit * along) / radius

    for copy in trade:
        copy.wait_recv()
    keep_mine = jnp.full((2 * ROWS, WIDTH), odd, I32) == 0
    moved_ref[...] = jnp.where(keep_mine, cand[...].astype(F32), cand_in[...].astype(F32)).astype(BF16)
    mvlab_ref[...] = jnp.where(jnp.full((1, 128), odd, I32) == 0, clab[...], clab_in[...])

    for copy in swaps + trade:
        copy.wait_send()
    lax.fori_loop(1, 16, plane_sent, 0)

    def sent(j, _):
        sums_plane(j).wait_send()
        for p in (0, 1):
            ring2(p, j).wait_send()
        return 0

    lax.fori_loop(1, 16, sent, 0)
    for off in (1, 2, 3):
        sums_line(off).wait_send()
        for p in (0, 1):
            line_labels(p, off, False).wait_send()
    for off in (1, 3):
        for p in (0, 1):
            line_rows(p, off, False).wait_send()
            relay(p, off, False).wait_send()
            onward(p, off).wait_send()
            for half in (0, 1):
                ring1(p, off, half).wait_send()


def finish(
    step_ref, grad_ref, loss_ref, moved_ref, mvlab_ref, mlab_ref, mem_ref,
    grad_out, loss_out, lab_out, mem_out, buf, sem_in, sem_out,
):
    pieces, size = buf.shape[0], buf.shape[1]
    slot = step_ref[0] % SLOTS
    loads = [
        pltpu.make_async_copy(mem_ref.at[pl.ds(i * size, size)], buf.at[i], sem_in.at[i])
        for i in range(pieces)
    ]
    stores = [
        pltpu.make_async_copy(buf.at[i], mem_out.at[pl.ds(i * size, size)], sem_out.at[i])
        for i in range(pieces)
    ]
    for load in loads:
        load.start()
    grad_out[...] = grad_ref[...]
    rows = loss_ref.shape[0]
    diagonal = lax.broadcasted_iota(I32, (rows, 128), 0) == lax.broadcasted_iota(I32, (rows, 128), 1)
    loss_out[...] = jnp.sum(jnp.where(diagonal, loss_ref[...], 0.0), axis=0, keepdims=True)[:, :rows]
    lane = lax.broadcasted_iota(I32, (1, 128), 1) // (2 * ROWS)
    for i in range(KEYS_DEV // 128):
        here = pl.ds(i * 128, 128)
        lab_out[:, here] = jnp.where(
            lane + i * (64 // ROWS) == jnp.full((1, 128), slot, I32), mvlab_ref[...], mlab_ref[:, here]
        )
    per_piece = size // (2 * ROWS)
    for i in range(pieces):
        loads[i].wait()

        @pl.when(slot // per_piece == i)
        def _():
            at = pl.multiple_of((slot % per_piece) * (2 * ROWS), 2 * ROWS)
            buf[i, pl.ds(at, 2 * ROWS), :] = moved_ref[...]

        stores[i].start()
    for store in stores:
        store.wait()


def per_device(batch_rows, batch_labels, memory, memory_labels, keep_bits, step_index):
    local_rows = batch_rows.shape[0]
    vmem = pl.BlockSpec(memory_space=pltpu.VMEM)
    dma = pltpu.SemaphoreType.DMA
    memory_labels_row = memory_labels.reshape(1, KEYS_DEV)
    grad, loss, moved, moved_labels = pl.pallas_call(
        kernel,
        out_shape=(
            jax.ShapeDtypeStruct((local_rows, WIDTH), F32),
            jax.ShapeDtypeStruct((local_rows, 128), F32),
            jax.ShapeDtypeStruct((local_rows, WIDTH), BF16),
            jax.ShapeDtypeStruct((1, 128), I32),
        ),
        in_specs=[pl.BlockSpec(memory_space=pltpu.SMEM), vmem, vmem, vmem, vmem, pl.BlockSpec(memory_space=pl.ANY)],
        out_specs=(vmem, vmem, vmem, vmem),
        scratch_shapes=[
            pltpu.VMEM((2, KEYS_DEV, WIDTH), BF16),
            pltpu.VMEM((2, 1, KEYS_DEV), I32),
            pltpu.VMEM((2, 1, KEYS_DEV), I32),
            pltpu.VMEM((KEYS, WIDTH), BF16),
            pltpu.VMEM((1, KEYS), F32),
            pltpu.VMEM((2, 4, 4, 4, ROWS, WIDTH), BF16),
            pltpu.VMEM((2, 4, 4, 4, 1, 128), I32),
            pltpu.VMEM((2, 4, CHUNK, WIDTH), BF16),
            pltpu.VMEM((2, 4, CHUNK, 128), F32),
            pltpu.VMEM((2, 4, CHUNK, KEYS), BF16),
            pltpu.VMEM((2, CHUNK, 128), F32),
            pltpu.VMEM((3, 2, 4, 4, 128), F32),
            pltpu.VMEM((15, 2, 4, 4, 128), F32),
            pltpu.VMEM((3, 2, 4, 4, 128), F32),
            pltpu.VMEM((2, 4, 2, CHUNK, 128), F32),
            pltpu.VMEM((2, 3, CHUNK, WIDTH), F32),
            pltpu.VMEM((2, CHUNK, WIDTH), F32),
            pltpu.VMEM((2, 3, 2, 128, WIDTH), BF16),
            pltpu.VMEM((2, 2, 2, 128, WIDTH), BF16),
            pltpu.VMEM((2, 2, 128, WIDTH), BF16),
            pltpu.VMEM((2, 2, 128, WIDTH), F32),
            pltpu.VMEM((2, 16, ROWS, WIDTH), F32),
            pltpu.VMEM((2, 16, ROWS, WIDTH), BF16),
            pltpu.VMEM((2, 15, ROWS, WIDTH), BF16),
            pltpu.VMEM((2 * ROWS, WIDTH), BF16),
            pltpu.VMEM((2 * ROWS, WIDTH), BF16),
            pltpu.VMEM((1, 128), I32),
            pltpu.VMEM((1, 128), I32),
            dma,
            dma((2, 15)), dma((2, 15)), dma((2, 15)), dma((2, 15)),
            dma((2, 2)), dma((2, 2)), dma((2, 3)), dma((2, 3)), dma((2, 2)), dma((2, 2)),
            dma((15,)), dma((15,)), dma((3,)), dma((3,)),
            dma((2, 2)), dma((2, 2)), dma((2, 2, 2)), dma((2, 2, 2)), dma((2, 15)), dma((2, 15)),
            dma((3,)), dma((3,)), dma((2,)), dma((2,)),
        ],
        compiler_params=pltpu.CompilerParams(
            collective_id=0, has_side_effects=True, vmem_limit_bytes=60 * 1024 * 1024
        ),
        name="xbm",
    )(
        step_index,
        batch_rows,
        batch_labels.reshape(1, local_rows),
        memory_labels_row,
        keep_bits.reshape(1, KEYS_DEV),
        memory,
    )
    smem, hbm = pl.BlockSpec(memory_space=pltpu.SMEM), pl.BlockSpec(memory_space=pl.ANY)
    pieces = 4
    grad, loss_row, new_labels, new_memory = pl.pallas_call(
        finish,
        out_shape=(
            jax.ShapeDtypeStruct((local_rows, WIDTH), F32),
            jax.ShapeDtypeStruct((1, local_rows), F32),
            jax.ShapeDtypeStruct((1, KEYS_DEV), I32),
            jax.ShapeDtypeStruct((KEYS_DEV, WIDTH), BF16),
        ),
        in_specs=[smem, vmem, vmem, vmem, vmem, vmem, hbm],
        out_specs=(vmem, vmem, vmem, hbm),
        scratch_shapes=[
            pltpu.VMEM((pieces, KEYS_DEV // pieces, WIDTH), BF16), dma((pieces,)), dma((pieces,)),
        ],
        name="finish",
    )(step_index, grad, loss, moved, moved_labels, memory_labels_row, memory)
    return grad, loss_row.reshape(local_rows), new_memory, new_labels.reshape(KEYS_DEV)


def solution(mesh):
    rows = P(("grp", "dev"), None)
    flat = P(("grp", "dev"))
    return jax.shard_map(
        per_device,
        mesh=mesh,
        in_specs=(rows, flat, rows, flat, flat, P()),
        out_specs=(rows, flat, rows, flat),
        check_vma=False,
    )
```

```python
import functools
import math

import jax
import jax.numpy as jnp
from jax import lax
from jax.experimental import pallas as pl
from jax.experimental.pallas import tpu as pltpu
from jax.sharding import PartitionSpec as P

F32, BF16, I32 = jnp.float32, jnp.bfloat16, jnp.int32
MESH = pl.DeviceIdType.MESH
LOG2E = math.log2(math.e)
EXP_NEG = math.exp(-25.0)
EXP_POS = math.exp(1.0)

ROWS = 16
CHUNK = 256
WIDTH = 512
KEYS_DEV = 2048
KEYS = 4096
OTHERS = (10, 6, 14, 9, 11, 2, 8, 5, 7, 13, 15, 1, 3, 4, 12)
SLOTS = KEYS_DEV // (2 * ROWS)


def column(row):
    return jnp.transpose(jnp.broadcast_to(row, (128, 128)))


def unit_scale(values):
    return lax.rsqrt(jnp.sum(values * values, axis=1, keepdims=True) + 1e-06)


def kernel(
    step_hbm, batch_hbm, blab_hbm, mlab_ref, keep_ref, mem_ref,
    grad_ref, loss_ref, moved_ref, mvlab_ref,
    step_ref, batch_ref, blab_ref,
    mraw, klraw, kpraw, keys, klab, raw, labs, an, labc, terms, acc, sums, sums_in, sums_z, den,
    pair, gown, sb1, rb1, hb, gr, g1, sb2, rb2, cand, cand_in, clab, clab_in,
    mem_sem, in_sem, pl_s, pl_r, pll_s, pll_r, ln_s, ln_r, lnl_s, lnl_r, fw_s, fw_r,
    as_s, as_r, az_s, az_r, h1_s, h1_r, r1_s, r1_r, r2_s, r2_r, pt_s, pt_r, bt_s, bt_r,
):
    n_dev = lax.axis_size("dev")
    me = lax.axis_index("grp") * n_dev + lax.axis_index("dev")
    core = me % 2
    chip = me // 2
    at = (chip // 16, (chip // 4) % 4, chip % 4)

    def device(index):
        return (index // n_dev, index % n_dev)

    even = core == 0
    sx, sy, sz = ([(at[a] + d) % 4 for d in range(4)] for a in range(3))
    grp_x, grp_y = [2 * v for v in sx], [v // 2 for v in sy]
    dev_y, dev_z = [8 * (v % 2) for v in sy], [2 * v + core for v in sz]
    along_x = [(grp_x[d] + grp_y[0], dev_y[0]) for d in range(4)]
    along_y = [(grp_x[0] + grp_y[d], dev_y[d]) for d in range(4)]
    mid1 = [tuple(jnp.where(even, a, b) for a, b in zip(along_x[d], along_y[d])) for d in range(4)]
    last1 = [tuple(jnp.where(even, a, b) for a, b in zip(along_y[d], along_x[d])) for d in range(4)]
    places = (
        (sz, sy, sx),
        ([jnp.where(even, a, b) for a, b in zip(sy, sx)], [jnp.where(even, a, b) for a, b in zip(sx, sy)], sz),
    )

    def chip_at(dx, dy, dz):
        return grp_x[dx] + grp_y[dy], dev_y[dy] + dev_z[dz]

    def peer(p, dl, dm, df):
        if not isinstance(p, int):
            return tuple(jnp.where(p == 0, a, b) for a, b in zip(peer(0, dl, dm, df), peer(1, dl, dm, df)))
        if p == 0:
            return chip_at(df, dm, dl)
        grp, dev = last1[dl] if dl else mid1[dm]
        return grp, dev + dev_z[df]

    def place(p):
        if isinstance(p, int):
            return tuple(axis[0] for axis in places[p])
        return tuple(jnp.where(p == 0, a[0], b[0]) for a, b in zip(*places))

    partner = device(me + 1 - 2 * core)

    def remote(src, dst, send, recv, to):
        return pltpu.make_async_remote_copy(
            src_ref=src, dst_ref=dst, send_sem=send, recv_sem=recv, device_id=to, device_id_type=MESH
        )

    own_mem = pltpu.make_async_copy(mem_ref, mraw.at[0], mem_sem)
    own_mem.start()
    small = (
        pltpu.make_async_copy(blab_hbm, blab_ref, in_sem.at[0]),
        pltpu.make_async_copy(batch_hbm, batch_ref, in_sem.at[1]),
        pltpu.make_async_copy(step_hbm, step_ref, in_sem.at[2]),
        pltpu.make_async_copy(mlab_ref, klraw.at[0], in_sem.at[3]),
        pltpu.make_async_copy(keep_ref, kpraw.at[0], in_sem.at[4]),
    )
    blocks = []
    for p in (0, 1):
        l, m, f = place(p)
        blocks.append(
            pltpu.make_async_copy(
                batch_hbm.at[pl.ds(p * ROWS, ROWS)], raw.at[p, l, m, f], in_sem.at[5 + p]
            )
        )
    for copy in (*small, *blocks):
        copy.start()

    barrier = pltpu.get_barrier_semaphore()
    def greet(p, dl, dm, df):
        pl.semaphore_signal(barrier, inc=1, device_id=peer(p, dl, dm, df), device_id_type=MESH)

    for j in OTHERS:
        greet(0, 0, j // 4, j % 4)
    for j in OTHERS:
        if j // 4 and j % 4:
            greet(1, 0, j // 4, j % 4)
    for off in (1, 2, 3):
        greet(0, off, 0, 0)
    pl.semaphore_signal(barrier, inc=1, device_id=partner, device_id_type=MESH)
    for copy in (*small, *blocks):
        copy.wait()
    for i in range(4):
        clab[:, 2 * ROWS * i : 2 * ROWS * (i + 1)] = blab_ref[...]
    for p in (0, 1):
        l, m, f = place(p)
        labs[p, l, m, f] = clab[...]
    pl.semaphore_wait(barrier, 28)

    def to_plane(p, j, back):
        dm, df = j // 4, j % 4
        l, middle, first = places[p][0][0], places[p][1], places[p][2]
        m, f = (middle[-dm % 4], first[-df % 4]) if back else (middle[0], first[0])
        rows, labels, to = raw.at[p, l, m, f], labs.at[p, l, m, f], peer(p, 0, dm, df)
        return (
            remote(rows, rows, pl_s.at[p, j - 1], pl_r.at[p, j - 1], to),
            remote(labels, labels, pll_s.at[p, j - 1], pll_r.at[p, j - 1], to),
        )

    def plane_start():
        for j in OTHERS:
            for p in (0, 1):
                for copy in to_plane(p, j, False):
                    copy.start()

    def plane_recv():
        for j in OTHERS:
            for p in (0, 1):
                for copy in to_plane(p, j, True):
                    copy.wait_recv()

    def plane_sent():
        for j in OTHERS:
            for p in (0, 1):
                for copy in to_plane(p, j, False):
                    copy.wait_send()

    def line_rows(p, off, back):
        l = place(p)[0]
        if back:
            l = (l + 4 - off) % 4
        rows = raw.at[p, l]
        return remote(rows, rows, ln_s.at[p, off // 2], ln_r.at[p, off // 2], peer(p, off, 0, 0))

    def line_labels(p, off, back):
        l = place(p)[0]
        if back:
            l = (l + 4 - off) % 4
        labels = labs.at[p, l]
        return remote(labels, labels, lnl_s.at[p, off - 1], lnl_r.at[p, off - 1], peer(p, off, 0, 0))

    def relay(p, off, back):
        l = place(p)[0]
        l = (l + (2 if back else 4 - off)) % 4
        half = raw.at[p, l, pl.ds(0 if off == 1 else 2, 2)]
        return remote(half, half, fw_s.at[p, off // 2], fw_r.at[p, off // 2], peer(p, off, 0, 0))

    plane_start()
    swaps = (
        remote(mem_ref, mraw.at[1], pt_s.at[0], pt_r.at[0], partner),
        remote(mlab_ref, klraw.at[1], pt_s.at[1], pt_r.at[1], partner),
        remote(keep_ref, kpraw.at[1], pt_s.at[2], pt_r.at[2], partner),
    )
    for copy in swaps:
        copy.start()

    def normalize_memory(half):
        def block(i, _):
            row = pl.multiple_of(i * 128, 128)
            kept = kpraw[half, :, pl.ds(row, 128)] > 0
            klab[:, pl.ds(pl.multiple_of(half * KEYS_DEV + row, 128), 128)] = jnp.where(
                kept, klraw[half, :, pl.ds(row, 128)], -1
            ).astype(F32)
            values = mraw[half, pl.ds(row, 128), :].astype(F32)
            scale = unit_scale(values) * column(jnp.where(kept, 1.0, 0.0))[:, 0:1]
            keys[pl.ds(pl.multiple_of(half * KEYS_DEV + row, 128), 128), :] = (values * scale).astype(BF16)
            return 0

        lax.fori_loop(0, KEYS_DEV // 128, block, 0)

    own_mem.wait()
    normalize_memory(0)
    plane_recv()
    for p in (1, 0):
        for off in (1, 3):
            line_rows(p, off, False).start()
        for off in (1, 3, 2):
            line_labels(p, off, False).start()
    for copy in swaps:
        copy.wait_recv()
    normalize_memory(1)

    dropped = float(KEYS) - jnp.sum(
        jnp.where(kpraw[...] > 0, 1.0, 0.0).reshape(2, KEYS_DEV), axis=(0, 1), keepdims=True
    )

    def prepare(p, l):
        values = raw[p, l].reshape(CHUNK, WIDTH).astype(F32)
        an[p, l] = (values * unit_scale(values)).astype(BF16)
        pages = labs[p, l].reshape(16, 128).astype(F32)
        wide = jnp.transpose(jnp.concatenate([pages] * 8, axis=0))
        mine = jnp.where(jnp.full((ROWS, 128), p, I32) == 0, wide[:ROWS], wide[ROWS : 2 * ROWS])
        for b in range(16):
            labc[p, l, pl.ds(b * ROWS, ROWS), :] = jnp.broadcast_to(mine[:, b : b + 1], (ROWS, 128))

    def score(p, l):
        s = lax.dot_general(
            an[p, l], keys[...], (((1,), (1,)), ((), ())), preferred_element_type=F32
        )
        labels = labc[p, l]
        all_sum = jnp.zeros((CHUNK, 128), F32)
        pos_sum = jnp.zeros((CHUNK, 128), F32)
        for j in range(0, KEYS, 128):
            same = labels == klab[:, j : j + 128]
            e = jnp.exp2(s[:, j : j + 128] * jnp.where(same, -2.0 * LOG2E, 50.0 * LOG2E))
            all_sum = all_sum + e
            pos_sum = pos_sum + jnp.where(same, e, 0.0)
            terms[p, l, :, j : j + 128] = e.astype(BF16)
        acc[0], acc[1] = all_sum, pos_sum
        for h in (0, 1):
            half = pl.ds(h * 128, 128)
            total = jnp.sum(jnp.transpose(acc[0, half, :]), axis=0, keepdims=True)
            pos = jnp.sum(jnp.transpose(acc[1, half, :]), axis=0, keepdims=True)
            sums[0, p, l, pl.ds(h, 1), :] = total - pos - dropped
            sums[0, p, l, pl.ds(2 + h, 1), :] = pos

    def visit(i, _):
        early_piece = jnp.logical_or(jnp.logical_or(i == 1, i == 2), jnp.logical_or(i == 3, i == 6))
        p = jnp.where(early_piece, 1, 0)
        off = jnp.where(i < 2, 0, jnp.where(i > 5, 2, jnp.where(i % 2 == 0, 1, 3)))
        here = (place(p)[0] + 4 - off) % 4

        @pl.when(jnp.logical_or(i == 2, i == 4))
        def _():
            for off in (1, 3):
                line_rows(p, off, True).wait_recv()
                relay(p, off, False).start()
                line_labels(p, off, True).wait_recv()

        @pl.when(i > 5)
        def _():
            for off in (1, 3):
                relay(p, off, True).wait_recv()
            line_labels(p, 2, True).wait_recv()

        prepare(p, here)
        score(p, here)
        return 0

    lax.fori_loop(0, 8, visit, 0)

    def part(p, l, weight):
        labels = labc[p, l]
        parts = []
        for j in range(0, KEYS, 128):
            same = labels == klab[:, j : j + 128]
            parts.append(weight(same, terms[p, l, :, j : j + 128].astype(F32)).astype(BF16))
        return jnp.dot(jnp.concatenate(parts, axis=1), keys[...], preferred_element_type=F32)

    def early(i):
        return i % 2, jnp.where(i == 2, 1, 2)

    def alone(i):
        p, off = early(i)
        l = (place(p)[0] + off) % 4
        pair[0, i] = part(p, l, lambda same, e: jnp.where(same, 0.0, e))
        pair[1, i] = part(p, l, lambda same, e: jnp.where(same, e, 0.0))

    def sums_plane(j):
        return remote(
            sums.at[0], sums_in.at[j - 1], as_s.at[j - 1], as_r.at[j - 1], chip_at(j % 4, j // 4, 0)
        )

    def sums_line(off):
        return remote(
            sums.at[1], sums_z.at[off - 1], az_s.at[off - 1], az_r.at[off - 1], chip_at(0, 0, off)
        )

    def add_up(i, _):
        @pl.when(i == 0)
        def _():
            for j in OTHERS:
                sums_plane(j).start()

        alone(i)

        @pl.when(i == 1)
        def _():
            for j in OTHERS:
                sums_plane(j).wait_recv()
            total = sums[0]
            for j in range(15):
                total = total + sums_in[j]
            sums[1] = total
            for off in (1, 3, 2):
                sums_line(off).start()

        return 0

    lax.fori_loop(0, 3, add_up, 0)
    for off in (1, 2, 3):
        sums_line(off).wait_recv()
    sums[2] = sums[1] + sums_z[0] + sums_z[1] + sums_z[2]

    def onward(p, off):
        side = off // 2
        return remote(
            sb1.at[p, 2, side], hb.at[p, side], h1_s.at[p, side], h1_r.at[p, side], peer(p, off, 0, 0)
        )

    def ring1(p, off, half):
        side = off // 2
        return remote(
            sb1.at[p, side, half], rb1.at[p, side, half],
            r1_s.at[p, side, half], r1_r.at[p, side, half], peer(p, off, 0, 0),
        )

    def dispatch(p, off, g):
        side = off // 2
        gr[p, side] = jnp.where(jnp.full((128, WIDTH), side, I32) == 0, g[:128], g[128:])
        sb1[p, side, 1 - side] = jnp.where(
            jnp.full((128, WIDTH), side, I32) == 0, g[128:], g[:128]
        ).astype(BF16)
        ring1(p, off, 1 - side).start()

    def complete(p, off):
        side = off // 2
        onward(p, off).wait_recv()
        sb1[p, side, side] = (gr[p, side] + hb[p, side].astype(F32)).astype(BF16)
        ring1(p, off, side).start()

    def weights(p, l):
        for h in (0, 1):
            half = pl.ds(h * 128, 128)
            den[p, l, 0, half, :] = column(1.0 + EXP_NEG * sums[2, p, l, pl.ds(h, 1), :])
            den[p, l, 1, half, :] = column(1.0 + EXP_POS * sums[2, p, l, pl.ds(2 + h, 1), :])
        return EXP_NEG / den[p, l, 0], -EXP_POS / den[p, l, 1]

    def ready(i):
        p, off = early(i)
        neg, pos = weights(p, (place(p)[0] + off) % 4)
        return jnp.concatenate(
            [
                pair[0, i, :, j : j + 128] * neg + pair[1, i, :, j : j + 128] * pos
                for j in range(0, WIDTH, 128)
            ],
            axis=1,
        )

    def push_early(p, _):
        sb1[p, 2] = ready(p).astype(BF16).reshape(2, 128, WIDTH)
        for off in (1, 3):
            onward(p, off).start()
        return 0

    lax.fori_loop(0, 2, push_early, 0)
    dispatch(0, 1, ready(2))

    def push(i, _):
        p, off = (i + 1) % 2, jnp.where(i == 0, 1, jnp.where(i < 3, 3, 0))
        l = (place(p)[0] + off) % 4
        neg, pos = weights(p, l)
        gown[p] = part(p, l, lambda same, e: e * jnp.where(same, pos, neg))

        @pl.when(i == 0)
        def _():
            dispatch(1, 1, gown[1])

        @pl.when(i == 1)
        def _():
            dispatch(0, 3, gown[0])
            complete(1, 1)

        @pl.when(i == 2)
        def _():
            dispatch(1, 3, gown[1])
            complete(0, 1)
            complete(0, 3)
            complete(1, 3)

        return 0

    lax.fori_loop(0, 5, push, 0)

    def ring2(p, j):
        dm, df = j // 4, j % 4
        block = places[p][1][dm] * 4 + places[p][2][df]
        return remote(
            sb2.at[p, block], rb2.at[p, j - 1], r2_s.at[p, j - 1], r2_r.at[p, j - 1], peer(p, 0, dm, df)
        )

    for p in (0, 1):
        for off in (1, 3):
            for half in (0, 1):
                ring1(p, off, half).wait_recv()
        g1[p] = (
            gown[p].reshape(2, 128, WIDTH) + rb1[p, 0].astype(F32) + rb1[p, 1].astype(F32)
        ).reshape(16, ROWS, WIDTH)
        sb2[p] = g1[p].astype(BF16)

        for j in OTHERS:
            ring2(p, j).start()

    step = step_ref[0]
    odd = step % 2
    mate = me + 1 - 2 * core
    asker = jnp.where(odd == 0, me, mate)
    block = ((asker + 1048576 - step) % 128) // 2
    wanted = jnp.full((ROWS, WIDTH), block, I32)
    wanted_row = jnp.full((1, 128), block, I32)

    def find(q, found):
        qx, qy, qz = q // 16, (q // 4) % 4, q % 4
        pick = wanted == q
        upper = an[0, qz, pl.ds(pl.multiple_of((qy * 4 + qx) * ROWS, ROWS), ROWS), :].astype(F32)
        ql, qm = jnp.where(core == 0, qy, qx), jnp.where(core == 0, qx, qy)
        lower = an[1, ql, pl.ds(pl.multiple_of((qm * 4 + qz) * ROWS, ROWS), ROWS), :].astype(F32)
        return (
            jnp.where(pick, upper, found[0]),
            jnp.where(pick, lower, found[1]),
            jnp.where(wanted_row == q, labs[0, qz, qy, qx], found[2]),
        )

    nothing = jnp.zeros((ROWS, WIDTH), F32)
    upper, lower, label_row = lax.fori_loop(
        0, 64, find, (nothing, nothing, jnp.zeros((1, 128), I32))
    )
    cand[pl.ds(0, ROWS), :] = upper.astype(BF16)
    cand[pl.ds(ROWS, ROWS), :] = lower.astype(BF16)
    clab[...] = label_row
    trade = (
        remote(cand, cand_in, bt_s.at[0], bt_r.at[0], partner),
        remote(clab, clab_in, bt_s.at[1], bt_r.at[1], partner),
    )
    for copy in trade:
        copy.start()

    for p in (0, 1):
        l, m, f = place(p)
        own = pl.ds(pl.multiple_of((m * 4 + f) * ROWS, ROWS), ROWS)
        mine = pl.ds(p * ROWS, ROWS)
        loss_ref[mine, :] = jnp.log(den[p, l, 1, own, :]) / 2.0 + jnp.log(den[p, l, 0, own, :]) / 50.0
    for p in (0, 1):
        l, m, f = place(p)

        for j in OTHERS:
            ring2(p, j).wait_recv()
        grad_unit = g1[p, m * 4 + f]
        for j in range(15):
            grad_unit = grad_unit + rb2[p, j].astype(F32)
        values = batch_ref[pl.ds(p * ROWS, ROWS), :].astype(F32)
        radius = jnp.sqrt(jnp.sum(values * values, axis=1, keepdims=True) + 1e-06)
        unit = values / radius
        along = jnp.sum(unit * grad_unit, axis=1, keepdims=True)
        grad_ref[pl.ds(p * ROWS, ROWS), :] = (grad_unit - unit * along) / radius

    for copy in trade:
        copy.wait_recv()
    keep_mine = jnp.full((2 * ROWS, WIDTH), odd, I32) == 0
    moved_ref[...] = jnp.where(keep_mine, cand[...].astype(F32), cand_in[...].astype(F32)).astype(BF16)
    mvlab_ref[...] = jnp.where(jnp.full((1, 128), odd, I32) == 0, clab[...], clab_in[...])

    for copy in swaps + trade:
        copy.wait_send()
    plane_sent()

    for j in OTHERS:
        sums_plane(j).wait_send()
        for p in (0, 1):
            ring2(p, j).wait_send()
    for off in (1, 2, 3):
        sums_line(off).wait_send()
        for p in (0, 1):
            line_labels(p, off, False).wait_send()
    for off in (1, 3):
        for p in (0, 1):
            line_rows(p, off, False).wait_send()
            relay(p, off, False).wait_send()
            onward(p, off).wait_send()
            for half in (0, 1):
                ring1(p, off, half).wait_send()


def finish(
    step_hbm, grad_hbm, loss_hbm, moved_hbm, mvlab_hbm, mlab_hbm, mem_ref,
    grad_out, loss_out, lab_out, mem_out,
    step_ref, grad, loss_in, moved, mvlab, mlab, loss, labels, buf, small_sem, done_sem, sem_in, sem_out,
):
    pieces, size = buf.shape[0], buf.shape[1]
    loads = [
        pltpu.make_async_copy(mem_ref.at[pl.ds(i * size, size)], buf.at[i], sem_in.at[i])
        for i in range(pieces)
    ]
    stores = [
        pltpu.make_async_copy(buf.at[i], mem_out.at[pl.ds(i * size, size)], sem_out.at[i])
        for i in range(pieces)
    ]
    pairs = (
        (step_hbm, step_ref), (moved_hbm, moved), (mvlab_hbm, mvlab), (mlab_hbm, mlab),
        (loss_hbm, loss_in), (grad_hbm, grad),
    )
    small = [pltpu.make_async_copy(a, b, small_sem.at[i]) for i, (a, b) in enumerate(pairs)]
    results = [
        pltpu.make_async_copy(a, b, done_sem.at[i])
        for i, (a, b) in enumerate(((loss, loss_out), (labels, lab_out), (grad, grad_out)))
    ]
    for copy in (*small[:2], *loads, *small[2:]):
        copy.start()
    small[0].wait()
    small[1].wait()
    slot = step_ref[0] % SLOTS
    per_piece = size // (2 * ROWS)
    for i in range(pieces):
        loads[i].wait()

        @pl.when(slot // per_piece == i)
        def _():
            at = pl.multiple_of((slot % per_piece) * (2 * ROWS), 2 * ROWS)
            buf[i, pl.ds(at, 2 * ROWS), :] = moved[...]

        stores[i].start()
    for copy in small[2:]:
        copy.wait()
    results[2].start()
    rows = loss_in.shape[0]
    diagonal = lax.broadcasted_iota(I32, (rows, 128), 0) == lax.broadcasted_iota(I32, (rows, 128), 1)
    loss[...] = jnp.sum(jnp.where(diagonal, loss_in[...], 0.0), axis=0, keepdims=True)[:, :rows]
    results[0].start()
    lane = lax.broadcasted_iota(I32, (1, 128), 1) // (2 * ROWS)
    for i in range(KEYS_DEV // 128):
        here = pl.ds(i * 128, 128)
        labels[:, here] = jnp.where(
            lane + i * (64 // ROWS) == jnp.full((1, 128), slot, I32), mvlab[...], mlab[:, here]
        )
    results[1].start()
    for copy in (*stores, *results):
        copy.wait()


def per_device(batch_rows, batch_labels, memory, memory_labels, keep_bits, step_index):
    local_rows = batch_rows.shape[0]
    vmem, hbm = pl.BlockSpec(memory_space=pltpu.VMEM), pl.BlockSpec(memory_space=pl.ANY)
    dma = pltpu.SemaphoreType.DMA
    memory_labels_row = memory_labels.reshape(1, KEYS_DEV)
    grad, loss, moved, moved_labels = pl.pallas_call(
        kernel,
        out_shape=(
            jax.ShapeDtypeStruct((local_rows, WIDTH), F32),
            jax.ShapeDtypeStruct((local_rows, 128), F32),
            jax.ShapeDtypeStruct((local_rows, WIDTH), BF16),
            jax.ShapeDtypeStruct((1, 128), I32),
        ),
        in_specs=[hbm] * 6,
        out_specs=(vmem, vmem, vmem, vmem),
        scratch_shapes=[
            pltpu.SMEM((1,), I32),
            pltpu.VMEM((2 * ROWS, WIDTH), BF16),
            pltpu.VMEM((1, 2 * ROWS), I32),
            pltpu.VMEM((2, KEYS_DEV, WIDTH), BF16),
            pltpu.VMEM((2, 1, KEYS_DEV), I32),
            pltpu.VMEM((2, 1, KEYS_DEV), I32),
            pltpu.VMEM((KEYS, WIDTH), BF16),
            pltpu.VMEM((1, KEYS), F32),
            pltpu.VMEM((2, 4, 4, 4, ROWS, WIDTH), BF16),
            pltpu.VMEM((2, 4, 4, 4, 1, 128), I32),
            pltpu.VMEM((2, 4, CHUNK, WIDTH), BF16),
            pltpu.VMEM((2, 4, CHUNK, 128), F32),
            pltpu.VMEM((2, 4, CHUNK, KEYS), BF16),
            pltpu.VMEM((2, CHUNK, 128), F32),
            pltpu.VMEM((3, 2, 4, 4, 128), F32),
            pltpu.VMEM((15, 2, 4, 4, 128), F32),
            pltpu.VMEM((3, 2, 4, 4, 128), F32),
            pltpu.VMEM((2, 4, 2, CHUNK, 128), F32),
            pltpu.VMEM((2, 3, CHUNK, WIDTH), F32),
            pltpu.VMEM((2, CHUNK, WIDTH), F32),
            pltpu.VMEM((2, 3, 2, 128, WIDTH), BF16),
            pltpu.VMEM((2, 2, 2, 128, WIDTH), BF16),
            pltpu.VMEM((2, 2, 128, WIDTH), BF16),
            pltpu.VMEM((2, 2, 128, WIDTH), F32),
            pltpu.VMEM((2, 16, ROWS, WIDTH), F32),
            pltpu.VMEM((2, 16, ROWS, WIDTH), BF16),
            pltpu.VMEM((2, 15, ROWS, WIDTH), BF16),
            pltpu.VMEM((2 * ROWS, WIDTH), BF16),
            pltpu.VMEM((2 * ROWS, WIDTH), BF16),
            pltpu.VMEM((1, 128), I32),
            pltpu.VMEM((1, 128), I32),
            dma,
            dma((7,)),
            dma((2, 15)), dma((2, 15)), dma((2, 15)), dma((2, 15)),
            dma((2, 2)), dma((2, 2)), dma((2, 3)), dma((2, 3)), dma((2, 2)), dma((2, 2)),
            dma((15,)), dma((15,)), dma((3,)), dma((3,)),
            dma((2, 2)), dma((2, 2)), dma((2, 2, 2)), dma((2, 2, 2)), dma((2, 15)), dma((2, 15)),
            dma((3,)), dma((3,)), dma((2,)), dma((2,)),
        ],
        compiler_params=pltpu.CompilerParams(
            collective_id=0, has_side_effects=True, vmem_limit_bytes=60 * 1024 * 1024
        ),
        name="xbm",
    )(
        step_index,
        batch_rows,
        batch_labels.reshape(1, local_rows),
        memory_labels_row,
        keep_bits.reshape(1, KEYS_DEV),
        memory,
    )
    pieces = 4
    grad, loss_row, new_labels, new_memory = pl.pallas_call(
        finish,
        out_shape=(
            jax.ShapeDtypeStruct((local_rows, WIDTH), F32),
            jax.ShapeDtypeStruct((1, local_rows), F32),
            jax.ShapeDtypeStruct((1, KEYS_DEV), I32),
            jax.ShapeDtypeStruct((KEYS_DEV, WIDTH), BF16),
        ),
        in_specs=[hbm] * 7,
        out_specs=(hbm,) * 4,
        scratch_shapes=[
            pltpu.SMEM((1,), I32),
            pltpu.VMEM((local_rows, WIDTH), F32),
            pltpu.VMEM((local_rows, 128), F32),
            pltpu.VMEM((local_rows, WIDTH), BF16),
            pltpu.VMEM((1, 128), I32),
            pltpu.VMEM((1, KEYS_DEV), I32),
            pltpu.VMEM((1, local_rows), F32),
            pltpu.VMEM((1, KEYS_DEV), I32),
            pltpu.VMEM((pieces, KEYS_DEV // pieces, WIDTH), BF16),
            dma((6,)), dma((3,)), dma((pieces,)), dma((pieces,)),
        ],
        name="finish",
    )(step_index, grad, loss, moved, moved_labels, memory_labels_row, memory)
    return grad, loss_row.reshape(local_rows), new_memory, new_labels.reshape(KEYS_DEV)


def solution(mesh):
    rows = P(("grp", "dev"), None)
    flat = P(("grp", "dev"))
    return jax.shard_map(
        per_device,
        mesh=mesh,
        in_specs=(rows, flat, rows, flat, flat, P()),
        out_specs=(rows, flat, rows, flat),
        check_vma=False,
    )
```

```python
import functools
import math

import jax
import jax.numpy as jnp
from jax import lax
from jax.experimental import pallas as pl
from jax.experimental.pallas import tpu as pltpu
from jax.sharding import PartitionSpec as P

F32, BF16, I32 = jnp.float32, jnp.bfloat16, jnp.int32
MESH = pl.DeviceIdType.MESH
LOG2E = math.log2(math.e)
EXP_NEG = math.exp(-25.0)
EXP_POS = math.exp(1.0)

ROWS = 16
CHUNK = 256
WIDTH = 512
KEYS_DEV = 2048
KEYS = 4096
OTHERS = (10, 6, 14, 9, 11, 2, 8, 5, 7, 13, 15, 1, 3, 4, 12)
SLOTS = KEYS_DEV // (2 * ROWS)


def column(row):
    return jnp.transpose(jnp.broadcast_to(row, (128, 128)))


def unit_scale(values):
    return lax.rsqrt(jnp.sum(values * values, axis=1, keepdims=True) + 1e-06)


def kernel(
    step_hbm, batch_hbm, blab_hbm, mlab_ref, keep_ref, mem_ref,
    grad_ref, loss_ref, moved_ref, mvlab_ref,
    step_ref, batch_ref, blab_ref,
    mraw, klraw, kpraw, keys, klab, raw, labs, an, labc, terms, acc, sums, sums_in, sums_z, den,
    pair, gown, sb1, rb1, hb, gr, g1, sb2, rb2, cand, cand_in, clab, clab_in,
    mem_sem, in_sem, pl_s, pl_r, pll_s, pll_r, ln_s, ln_r, lnl_s, lnl_r, fw_s, fw_r,
    as_s, as_r, az_s, az_r, h1_s, h1_r, r1_s, r1_r, r2_s, r2_r, pt_s, pt_r, bt_s, bt_r,
):
    n_dev = lax.axis_size("dev")
    me = lax.axis_index("grp") * n_dev + lax.axis_index("dev")
    core = me % 2
    chip = me // 2
    at = (chip // 16, (chip // 4) % 4, chip % 4)

    def device(index):
        return (index // n_dev, index % n_dev)

    even = core == 0
    sx, sy, sz = ([(at[a] + d) % 4 for d in range(4)] for a in range(3))
    grp_x, grp_y = [2 * v for v in sx], [v // 2 for v in sy]
    dev_y, dev_z = [8 * (v % 2) for v in sy], [2 * v + core for v in sz]
    along_x = [(grp_x[d] + grp_y[0], dev_y[0]) for d in range(4)]
    along_y = [(grp_x[0] + grp_y[d], dev_y[d]) for d in range(4)]
    mid1 = [tuple(jnp.where(even, a, b) for a, b in zip(along_x[d], along_y[d])) for d in range(4)]
    last1 = [tuple(jnp.where(even, a, b) for a, b in zip(along_y[d], along_x[d])) for d in range(4)]
    places = (
        (sz, sy, sx),
        ([jnp.where(even, a, b) for a, b in zip(sy, sx)], [jnp.where(even, a, b) for a, b in zip(sx, sy)], sz),
    )

    def chip_at(dx, dy, dz):
        return grp_x[dx] + grp_y[dy], dev_y[dy] + dev_z[dz]

    def peer(p, dl, dm, df):
        if not isinstance(p, int):
            return tuple(jnp.where(p == 0, a, b) for a, b in zip(peer(0, dl, dm, df), peer(1, dl, dm, df)))
        if p == 0:
            return chip_at(df, dm, dl)
        grp, dev = last1[dl] if dl else mid1[dm]
        return grp, dev + dev_z[df]

    def place(p):
        if isinstance(p, int):
            return tuple(axis[0] for axis in places[p])
        return tuple(jnp.where(p == 0, a[0], b[0]) for a, b in zip(*places))

    partner = device(me + 1 - 2 * core)

    def remote(src, dst, send, recv, to):
        return pltpu.make_async_remote_copy(
            src_ref=src, dst_ref=dst, send_sem=send, recv_sem=recv, device_id=to, device_id_type=MESH
        )

    own_mem = pltpu.make_async_copy(mem_ref, mraw.at[0], mem_sem)
    own_mem.start()
    small = (
        pltpu.make_async_copy(blab_hbm, blab_ref, in_sem.at[0]),
        pltpu.make_async_copy(batch_hbm, batch_ref, in_sem.at[1]),
        pltpu.make_async_copy(step_hbm, step_ref, in_sem.at[2]),
        pltpu.make_async_copy(mlab_ref, klraw.at[0], in_sem.at[3]),
        pltpu.make_async_copy(keep_ref, kpraw.at[0], in_sem.at[4]),
    )
    blocks = []
    for p in (0, 1):
        l, m, f = place(p)
        blocks.append(
            pltpu.make_async_copy(
                batch_hbm.at[pl.ds(p * ROWS, ROWS)], raw.at[p, l, m, f], in_sem.at[5 + p]
            )
        )
    for copy in (*small, *blocks):
        copy.start()

    barrier = pltpu.get_barrier_semaphore()
    def greet(p, dl, dm, df):
        pl.semaphore_signal(barrier, inc=1, device_id=peer(p, dl, dm, df), device_id_type=MESH)

    for j in OTHERS:
        greet(0, 0, j // 4, j % 4)
    for j in OTHERS:
        if j // 4 and j % 4:
            greet(1, 0, j // 4, j % 4)
    for off in (1, 2, 3):
        greet(0, off, 0, 0)
    pl.semaphore_signal(barrier, inc=1, device_id=partner, device_id_type=MESH)
    for copy in (*small, *blocks):
        copy.wait()
    for i in range(4):
        clab[:, 2 * ROWS * i : 2 * ROWS * (i + 1)] = blab_ref[...]
    for p in (0, 1):
        l, m, f = place(p)
        labs[p, l, m, f] = clab[...]
    pl.semaphore_wait(barrier, 28)

    def to_plane(p, j, back):
        dm, df = j // 4, j % 4
        l, middle, first = places[p][0][0], places[p][1], places[p][2]
        m, f = (middle[-dm % 4], first[-df % 4]) if back else (middle[0], first[0])
        rows, labels, to = raw.at[p, l, m, f], labs.at[p, l, m, f], peer(p, 0, dm, df)
        return (
            remote(rows, rows, pl_s.at[p, j - 1], pl_r.at[p, j - 1], to),
            remote(labels, labels, pll_s.at[p, j - 1], pll_r.at[p, j - 1], to),
        )

    def plane_start():
        for j in OTHERS:
            for p in (0, 1):
                for copy in to_plane(p, j, False):
                    copy.start()

    def plane_recv():
        for j in OTHERS:
            for p in (0, 1):
                for copy in to_plane(p, j, True):
                    copy.wait_recv()

    def plane_sent():
        for j in OTHERS:
            for p in (0, 1):
                for copy in to_plane(p, j, False):
                    copy.wait_send()

    def line_rows(p, off, back):
        l = place(p)[0]
        if back:
            l = (l + 4 - off) % 4
        rows = raw.at[p, l]
        return remote(rows, rows, ln_s.at[p, off // 2], ln_r.at[p, off // 2], peer(p, off, 0, 0))

    def line_labels(p, off, back):
        l = place(p)[0]
        if back:
            l = (l + 4 - off) % 4
        labels = labs.at[p, l]
        return remote(labels, labels, lnl_s.at[p, off - 1], lnl_r.at[p, off - 1], peer(p, off, 0, 0))

    def relay(p, off, back):
        l = place(p)[0]
        l = (l + (2 if back else 4 - off)) % 4
        half = raw.at[p, l, pl.ds(0 if off == 1 else 2, 2)]
        return remote(half, half, fw_s.at[p, off // 2], fw_r.at[p, off // 2], peer(p, off, 0, 0))

    plane_start()
    swaps = (
        remote(mem_ref, mraw.at[1], pt_s.at[0], pt_r.at[0], partner),
        remote(mlab_ref, klraw.at[1], pt_s.at[1], pt_r.at[1], partner),
        remote(keep_ref, kpraw.at[1], pt_s.at[2], pt_r.at[2], partner),
    )
    for copy in swaps:
        copy.start()

    def normalize_memory(half):
        def block(i, _):
            row = pl.multiple_of(i * 128, 128)
            kept = kpraw[half, :, pl.ds(row, 128)] > 0
            klab[:, pl.ds(pl.multiple_of(half * KEYS_DEV + row, 128), 128)] = jnp.where(
                kept, klraw[half, :, pl.ds(row, 128)], -1
            ).astype(F32)
            values = mraw[half, pl.ds(row, 128), :].astype(F32)
            scale = unit_scale(values) * column(jnp.where(kept, 1.0, 0.0))[:, 0:1]
            keys[pl.ds(pl.multiple_of(half * KEYS_DEV + row, 128), 128), :] = (values * scale).astype(BF16)
            return 0

        lax.fori_loop(0, KEYS_DEV // 128, block, 0, unroll=4)

    own_mem.wait()
    normalize_memory(0)
    for copy in swaps:
        copy.wait_recv()
    normalize_memory(1)
    plane_recv()
    for p in (1, 0):
        for off in (1, 3):
            line_rows(p, off, False).start()
        for off in (1, 3, 2):
            line_labels(p, off, False).start()

    dropped = float(KEYS) - jnp.sum(
        jnp.where(kpraw[...] > 0, 1.0, 0.0).reshape(2, KEYS_DEV), axis=(0, 1), keepdims=True
    )

    def prepare(p, l):
        values = raw[p, l].reshape(CHUNK, WIDTH).astype(F32)
        an[p, l] = (values * unit_scale(values)).astype(BF16)
        pages = labs[p, l].reshape(16, 128).astype(F32)
        wide = jnp.transpose(jnp.concatenate([pages] * 8, axis=0))
        mine = jnp.where(jnp.full((ROWS, 128), p, I32) == 0, wide[:ROWS], wide[ROWS : 2 * ROWS])
        for b in range(16):
            labc[p, l, pl.ds(b * ROWS, ROWS), :] = jnp.broadcast_to(mine[:, b : b + 1], (ROWS, 128))

    def score(p, l):
        s = lax.dot_general(
            an[p, l], keys[...], (((1,), (1,)), ((), ())), preferred_element_type=F32
        )
        labels = labc[p, l]
        all_sum = jnp.zeros((CHUNK, 128), F32)
        pos_sum = jnp.zeros((CHUNK, 128), F32)
        for j in range(0, KEYS, 128):
            same = labels == klab[:, j : j + 128]
            e = jnp.exp2(s[:, j : j + 128] * jnp.where(same, -2.0 * LOG2E, 50.0 * LOG2E))
            all_sum = all_sum + e
            pos_sum = pos_sum + jnp.where(same, e, 0.0)
            terms[p, l, :, j : j + 128] = e.astype(BF16)
        acc[0], acc[1] = all_sum, pos_sum
        for h in (0, 1):
            half = pl.ds(h * 128, 128)
            total = jnp.sum(jnp.transpose(acc[0, half, :]), axis=0, keepdims=True)
            pos = jnp.sum(jnp.transpose(acc[1, half, :]), axis=0, keepdims=True)
            sums[0, p, l, pl.ds(h, 1), :] = total - pos - dropped
            sums[0, p, l, pl.ds(2 + h, 1), :] = pos

    def visit(i, _):
        early_piece = jnp.logical_or(jnp.logical_or(i == 1, i == 2), jnp.logical_or(i == 3, i == 6))
        p = jnp.where(early_piece, 1, 0)
        off = jnp.where(i < 2, 0, jnp.where(i > 5, 2, jnp.where(i % 2 == 0, 1, 3)))
        here = (place(p)[0] + 4 - off) % 4

        @pl.when(jnp.logical_or(i == 2, i == 4))
        def _():
            for off in (1, 3):
                line_rows(p, off, True).wait_recv()
                relay(p, off, False).start()
                line_labels(p, off, True).wait_recv()

        @pl.when(i > 5)
        def _():
            for off in (1, 3):
                relay(p, off, True).wait_recv()
            line_labels(p, 2, True).wait_recv()

        prepare(p, here)
        score(p, here)
        return 0

    lax.fori_loop(0, 8, visit, 0)

    def part(p, l, weight):
        labels = labc[p, l]
        parts = []
        for j in range(0, KEYS, 128):
            same = labels == klab[:, j : j + 128]
            parts.append(weight(same, terms[p, l, :, j : j + 128].astype(F32)).astype(BF16))
        return jnp.dot(jnp.concatenate(parts, axis=1), keys[...], preferred_element_type=F32)

    def early(i):
        return i % 2, jnp.where(i == 2, 1, 2)

    def alone(i):
        p, off = early(i)
        l = (place(p)[0] + off) % 4
        pair[0, i] = part(p, l, lambda same, e: jnp.where(same, 0.0, e))
        pair[1, i] = part(p, l, lambda same, e: jnp.where(same, e, 0.0))

    def sums_plane(j):
        return remote(
            sums.at[0], sums_in.at[j - 1], as_s.at[j - 1], as_r.at[j - 1], chip_at(j % 4, j // 4, 0)
        )

    def sums_line(off):
        return remote(
            sums.at[1], sums_z.at[off - 1], az_s.at[off - 1], az_r.at[off - 1], chip_at(0, 0, off)
        )

    def add_up(i, _):
        @pl.when(i == 0)
        def _():
            for j in OTHERS:
                sums_plane(j).start()

        alone(i)

        @pl.when(i == 1)
        def _():
            for j in OTHERS:
                sums_plane(j).wait_recv()
            total = sums[0]
            for j in range(15):
                total = total + sums_in[j]
            sums[1] = total
            for off in (1, 3, 2):
                sums_line(off).start()

        return 0

    lax.fori_loop(0, 3, add_up, 0)
    for off in (1, 2, 3):
        sums_line(off).wait_recv()
    sums[2] = sums[1] + sums_z[0] + sums_z[1] + sums_z[2]

    def onward(p, off):
        side = off // 2
        return remote(
            sb1.at[p, 2, side], hb.at[p, side], h1_s.at[p, side], h1_r.at[p, side], peer(p, off, 0, 0)
        )

    def ring1(p, off, half):
        side = off // 2
        return remote(
            sb1.at[p, side, half], rb1.at[p, side, half],
            r1_s.at[p, side, half], r1_r.at[p, side, half], peer(p, off, 0, 0),
        )

    def dispatch(p, off, g):
        side = off // 2
        gr[p, side] = jnp.where(jnp.full((128, WIDTH), side, I32) == 0, g[:128], g[128:])
        sb1[p, side, 1 - side] = jnp.where(
            jnp.full((128, WIDTH), side, I32) == 0, g[128:], g[:128]
        ).astype(BF16)
        ring1(p, off, 1 - side).start()

    def complete(p, off):
        side = off // 2
        onward(p, off).wait_recv()
        sb1[p, side, side] = (gr[p, side] + hb[p, side].astype(F32)).astype(BF16)
        ring1(p, off, side).start()

    def weights(p, l):
        for h in (0, 1):
            half = pl.ds(h * 128, 128)
            den[p, l, 0, half, :] = column(1.0 + EXP_NEG * sums[2, p, l, pl.ds(h, 1), :])
            den[p, l, 1, half, :] = column(1.0 + EXP_POS * sums[2, p, l, pl.ds(2 + h, 1), :])
        return EXP_NEG / den[p, l, 0], -EXP_POS / den[p, l, 1]

    def ready(i):
        p, off = early(i)
        neg, pos = weights(p, (place(p)[0] + off) % 4)
        return jnp.concatenate(
            [
                pair[0, i, :, j : j + 128] * neg + pair[1, i, :, j : j + 128] * pos
                for j in range(0, WIDTH, 128)
            ],
            axis=1,
        )

    def push_early(p, _):
        sb1[p, 2] = ready(p).astype(BF16).reshape(2, 128, WIDTH)
        for off in (1, 3):
            onward(p, off).start()
        return 0

    lax.fori_loop(0, 2, push_early, 0)
    dispatch(0, 1, ready(2))

    def push(i, _):
        p, off = (i + 1) % 2, jnp.where(i == 0, 1, jnp.where(i < 3, 3, 0))
        l = (place(p)[0] + off) % 4
        neg, pos = weights(p, l)
        gown[p] = part(p, l, lambda same, e: e * jnp.where(same, pos, neg))

        @pl.when(i == 0)
        def _():
            dispatch(1, 1, gown[1])

        @pl.when(i == 1)
        def _():
            dispatch(0, 3, gown[0])
            complete(1, 1)

        @pl.when(i == 2)
        def _():
            dispatch(1, 3, gown[1])
            complete(0, 1)
            complete(0, 3)
            complete(1, 3)

        return 0

    lax.fori_loop(0, 5, push, 0)

    def ring2(p, j):
        dm, df = j // 4, j % 4
        block = places[p][1][dm] * 4 + places[p][2][df]
        return remote(
            sb2.at[p, block], rb2.at[p, j - 1], r2_s.at[p, j - 1], r2_r.at[p, j - 1], peer(p, 0, dm, df)
        )

    for p in (0, 1):
        for off in (1, 3):
            for half in (0, 1):
                ring1(p, off, half).wait_recv()
        g1[p] = (
            gown[p].reshape(2, 128, WIDTH) + rb1[p, 0].astype(F32) + rb1[p, 1].astype(F32)
        ).reshape(16, ROWS, WIDTH)
        sb2[p] = g1[p].astype(BF16)

        for j in OTHERS:
            ring2(p, j).start()

    step = step_ref[0]
    odd = step % 2
    mate = me + 1 - 2 * core
    asker = jnp.where(odd == 0, me, mate)
    block = ((asker + 1048576 - step) % 128) // 2
    wanted = jnp.full((ROWS, WIDTH), block, I32)
    wanted_row = jnp.full((1, 128), block, I32)

    def find(q, found):
        qx, qy, qz = q // 16, (q // 4) % 4, q % 4
        pick = wanted == q
        upper = an[0, qz, pl.ds(pl.multiple_of((qy * 4 + qx) * ROWS, ROWS), ROWS), :].astype(F32)
        ql, qm = jnp.where(core == 0, qy, qx), jnp.where(core == 0, qx, qy)
        lower = an[1, ql, pl.ds(pl.multiple_of((qm * 4 + qz) * ROWS, ROWS), ROWS), :].astype(F32)
        return (
            jnp.where(pick, upper, found[0]),
            jnp.where(pick, lower, found[1]),
            jnp.where(wanted_row == q, labs[0, qz, qy, qx], found[2]),
        )

    nothing = jnp.zeros((ROWS, WIDTH), F32)
    upper, lower, label_row = lax.fori_loop(
        0, 64, find, (nothing, nothing, jnp.zeros((1, 128), I32))
    )
    cand[pl.ds(0, ROWS), :] = upper.astype(BF16)
    cand[pl.ds(ROWS, ROWS), :] = lower.astype(BF16)
    clab[...] = label_row
    trade = (
        remote(cand, cand_in, bt_s.at[0], bt_r.at[0], partner),
        remote(clab, clab_in, bt_s.at[1], bt_r.at[1], partner),
    )
    for copy in trade:
        copy.start()

    for p in (0, 1):
        l, m, f = place(p)
        own = pl.ds(pl.multiple_of((m * 4 + f) * ROWS, ROWS), ROWS)
        mine = pl.ds(p * ROWS, ROWS)
        loss_ref[mine, :] = jnp.log(den[p, l, 1, own, :]) / 2.0 + jnp.log(den[p, l, 0, own, :]) / 50.0
    for p in (0, 1):
        l, m, f = place(p)

        for j in OTHERS:
            ring2(p, j).wait_recv()
        grad_unit = g1[p, m * 4 + f]
        for j in range(15):
            grad_unit = grad_unit + rb2[p, j].astype(F32)
        values = batch_ref[pl.ds(p * ROWS, ROWS), :].astype(F32)
        radius = jnp.sqrt(jnp.sum(values * values, axis=1, keepdims=True) + 1e-06)
        unit = values / radius
        along = jnp.sum(unit * grad_unit, axis=1, keepdims=True)
        grad_ref[pl.ds(p * ROWS, ROWS), :] = (grad_unit - unit * along) / radius

    for copy in trade:
        copy.wait_recv()
    keep_mine = jnp.full((2 * ROWS, WIDTH), odd, I32) == 0
    moved_ref[...] = jnp.where(keep_mine, cand[...].astype(F32), cand_in[...].astype(F32)).astype(BF16)
    mvlab_ref[...] = jnp.where(jnp.full((1, 128), odd, I32) == 0, clab[...], clab_in[...])

    for copy in swaps + trade:
        copy.wait_send()
    plane_sent()

    for j in OTHERS:
        sums_plane(j).wait_send()
        for p in (0, 1):
            ring2(p, j).wait_send()
    for off in (1, 2, 3):
        sums_line(off).wait_send()
        for p in (0, 1):
            line_labels(p, off, False).wait_send()
    for off in (1, 3):
        for p in (0, 1):
            line_rows(p, off, False).wait_send()
            relay(p, off, False).wait_send()
            onward(p, off).wait_send()
            for half in (0, 1):
                ring1(p, off, half).wait_send()


def finish(
    step_hbm, grad_hbm, loss_hbm, moved_hbm, mvlab_hbm, mlab_hbm, mem_ref,
    grad_out, loss_out, lab_out, mem_out,
    step_ref, grad, loss_in, moved, mvlab, mlab, loss, labels, buf, small_sem, done_sem, sem_in, sem_out,
):
    pieces, size = buf.shape[0], buf.shape[1]
    loads = [
        pltpu.make_async_copy(mem_ref.at[pl.ds(i * size, size)], buf.at[i], sem_in.at[i])
        for i in range(pieces)
    ]
    stores = [
        pltpu.make_async_copy(buf.at[i], mem_out.at[pl.ds(i * size, size)], sem_out.at[i])
        for i in range(pieces)
    ]
    pairs = (
        (step_hbm, step_ref), (moved_hbm, moved), (mvlab_hbm, mvlab), (mlab_hbm, mlab),
        (loss_hbm, loss_in), (grad_hbm, grad),
    )
    small = [pltpu.make_async_copy(a, b, small_sem.at[i]) for i, (a, b) in enumerate(pairs)]
    results = [
        pltpu.make_async_copy(a, b, done_sem.at[i])
        for i, (a, b) in enumerate(((loss, loss_out), (labels, lab_out), (grad, grad_out)))
    ]
    for copy in (*small[:2], *loads, *small[2:]):
        copy.start()
    small[0].wait()
    small[1].wait()
    slot = step_ref[0] % SLOTS
    per_piece = size // (2 * ROWS)
    for i in range(pieces):
        loads[i].wait()

        @pl.when(slot // per_piece == i)
        def _():
            at = pl.multiple_of((slot % per_piece) * (2 * ROWS), 2 * ROWS)
            buf[i, pl.ds(at, 2 * ROWS), :] = moved[...]

        stores[i].start()
    for copy in small[2:]:
        copy.wait()
    results[2].start()
    rows = loss_in.shape[0]
    diagonal = lax.broadcasted_iota(I32, (rows, 128), 0) == lax.broadcasted_iota(I32, (rows, 128), 1)
    loss[...] = jnp.sum(jnp.where(diagonal, loss_in[...], 0.0), axis=0, keepdims=True)[:, :rows]
    results[0].start()
    lane = lax.broadcasted_iota(I32, (1, 128), 1) // (2 * ROWS)
    for i in range(KEYS_DEV // 128):
        here = pl.ds(i * 128, 128)
        labels[:, here] = jnp.where(
            lane + i * (64 // ROWS) == jnp.full((1, 128), slot, I32), mvlab[...], mlab[:, here]
        )
    results[1].start()
    for copy in (*stores, *results):
        copy.wait()


def per_device(batch_rows, batch_labels, memory, memory_labels, keep_bits, step_index):
    local_rows = batch_rows.shape[0]
    vmem, hbm = pl.BlockSpec(memory_space=pltpu.VMEM), pl.BlockSpec(memory_space=pl.ANY)
    dma = pltpu.SemaphoreType.DMA
    memory_labels_row = memory_labels.reshape(1, KEYS_DEV)
    grad, loss, moved, moved_labels = pl.pallas_call(
        kernel,
        out_shape=(
            jax.ShapeDtypeStruct((local_rows, WIDTH), F32),
            jax.ShapeDtypeStruct((local_rows, 128), F32),
            jax.ShapeDtypeStruct((local_rows, WIDTH), BF16),
            jax.ShapeDtypeStruct((1, 128), I32),
        ),
        in_specs=[hbm] * 6,
        out_specs=(vmem, vmem, vmem, vmem),
        scratch_shapes=[
            pltpu.SMEM((1,), I32),
            pltpu.VMEM((2 * ROWS, WIDTH), BF16),
            pltpu.VMEM((1, 2 * ROWS), I32),
            pltpu.VMEM((2, KEYS_DEV, WIDTH), BF16),
            pltpu.VMEM((2, 1, KEYS_DEV), I32),
            pltpu.VMEM((2, 1, KEYS_DEV), I32),
            pltpu.VMEM((KEYS, WIDTH), BF16),
            pltpu.VMEM((1, KEYS), F32),
            pltpu.VMEM((2, 4, 4, 4, ROWS, WIDTH), BF16),
            pltpu.VMEM((2, 4, 4, 4, 1, 128), I32),
            pltpu.VMEM((2, 4, CHUNK, WIDTH), BF16),
            pltpu.VMEM((2, 4, CHUNK, 128), F32),
            pltpu.VMEM((2, 4, CHUNK, KEYS), BF16),
            pltpu.VMEM((2, CHUNK, 128), F32),
            pltpu.VMEM((3, 2, 4, 4, 128), F32),
            pltpu.VMEM((15, 2, 4, 4, 128), F32),
            pltpu.VMEM((3, 2, 4, 4, 128), F32),
            pltpu.VMEM((2, 4, 2, CHUNK, 128), F32),
            pltpu.VMEM((2, 3, CHUNK, WIDTH), F32),
            pltpu.VMEM((2, CHUNK, WIDTH), F32),
            pltpu.VMEM((2, 3, 2, 128, WIDTH), BF16),
            pltpu.VMEM((2, 2, 2, 128, WIDTH), BF16),
            pltpu.VMEM((2, 2, 128, WIDTH), BF16),
            pltpu.VMEM((2, 2, 128, WIDTH), F32),
            pltpu.VMEM((2, 16, ROWS, WIDTH), F32),
            pltpu.VMEM((2, 16, ROWS, WIDTH), BF16),
            pltpu.VMEM((2, 15, ROWS, WIDTH), BF16),
            pltpu.VMEM((2 * ROWS, WIDTH), BF16),
            pltpu.VMEM((2 * ROWS, WIDTH), BF16),
            pltpu.VMEM((1, 128), I32),
            pltpu.VMEM((1, 128), I32),
            dma,
            dma((7,)),
            dma((2, 15)), dma((2, 15)), dma((2, 15)), dma((2, 15)),
            dma((2, 2)), dma((2, 2)), dma((2, 3)), dma((2, 3)), dma((2, 2)), dma((2, 2)),
            dma((15,)), dma((15,)), dma((3,)), dma((3,)),
            dma((2, 2)), dma((2, 2)), dma((2, 2, 2)), dma((2, 2, 2)), dma((2, 15)), dma((2, 15)),
            dma((3,)), dma((3,)), dma((2,)), dma((2,)),
        ],
        compiler_params=pltpu.CompilerParams(
            collective_id=0, has_side_effects=True, vmem_limit_bytes=60 * 1024 * 1024
        ),
        name="xbm",
    )(
        step_index,
        batch_rows,
        batch_labels.reshape(1, local_rows),
        memory_labels_row,
        keep_bits.reshape(1, KEYS_DEV),
        memory,
    )
    pieces = 4
    grad, loss_row, new_labels, new_memory = pl.pallas_call(
        finish,
        out_shape=(
            jax.ShapeDtypeStruct((local_rows, WIDTH), F32),
            jax.ShapeDtypeStruct((1, local_rows), F32),
            jax.ShapeDtypeStruct((1, KEYS_DEV), I32),
            jax.ShapeDtypeStruct((KEYS_DEV, WIDTH), BF16),
        ),
        in_specs=[hbm] * 7,
        out_specs=(hbm,) * 4,
        scratch_shapes=[
            pltpu.SMEM((1,), I32),
            pltpu.VMEM((local_rows, WIDTH), F32),
            pltpu.VMEM((local_rows, 128), F32),
            pltpu.VMEM((local_rows, WIDTH), BF16),
            pltpu.VMEM((1, 128), I32),
            pltpu.VMEM((1, KEYS_DEV), I32),
            pltpu.VMEM((1, local_rows), F32),
            pltpu.VMEM((1, KEYS_DEV), I32),
            pltpu.VMEM((pieces, KEYS_DEV // pieces, WIDTH), BF16),
            dma((6,)), dma((3,)), dma((pieces,)), dma((pieces,)),
        ],
        name="finish",
    )(step_index, grad, loss, moved, moved_labels, memory_labels_row, memory)
    return grad, loss_row.reshape(local_rows), new_memory, new_labels.reshape(KEYS_DEV)


def solution(mesh):
    rows = P(("grp", "dev"), None)
    flat = P(("grp", "dev"))
    return jax.shard_map(
        per_device,
        mesh=mesh,
        in_specs=(rows, flat, rows, flat, flat, P()),
        out_specs=(rows, flat, rows, flat),
        check_vma=False,
    )
```

```python
import functools
import math

import jax
import jax.numpy as jnp
from jax import lax
from jax.experimental import pallas as pl
from jax.experimental.pallas import tpu as pltpu
from jax.sharding import PartitionSpec as P

F32, BF16, I32 = jnp.float32, jnp.bfloat16, jnp.int32
MESH = pl.DeviceIdType.MESH
LOG2E = math.log2(math.e)
EXP_NEG = math.exp(-25.0)
EXP_POS = math.exp(1.0)

ROWS = 16
CHUNK = 256
WIDTH = 512
KEYS_DEV = 2048
KEYS = 4096
OTHERS = (10, 6, 14, 9, 11, 2, 8, 5, 7, 13, 15, 1, 3, 4, 12)
SLOTS = KEYS_DEV // (2 * ROWS)


def column(row):
    return jnp.transpose(jnp.broadcast_to(row, (128, 128)))


def unit_scale(values):
    return lax.rsqrt(jnp.sum(values * values, axis=1, keepdims=True) + 1e-06)


def kernel(
    step_hbm, batch_hbm, blab_hbm, mlab_ref, keep_ref, mem_ref,
    grad_ref, loss_ref, moved_ref, mvlab_ref,
    step_ref, batch_ref, blab_ref,
    mraw, klraw, kpraw, keys, klab, raw, labs, an, labc, terms, acc, sums, sums_in, sums_z, den,
    pair, gown, sb1, rb1, hb, gr, g1, sb2, rb2, cand, cand_in, clab, clab_in,
    mem_sem, in_sem, pl_s, pl_r, pll_s, pll_r, ln_s, ln_r, lnl_s, lnl_r, fw_s, fw_r,
    as_s, as_r, az_s, az_r, h1_s, h1_r, r1_s, r1_r, r2_s, r2_r, pt_s, pt_r, bt_s, bt_r,
):
    n_dev = lax.axis_size("dev")
    me = lax.axis_index("grp") * n_dev + lax.axis_index("dev")
    core = me % 2
    chip = me // 2
    at = (chip // 16, (chip // 4) % 4, chip % 4)

    def device(index):
        return (index // n_dev, index % n_dev)

    even = core == 0
    sx, sy, sz = ([(at[a] + d) % 4 for d in range(4)] for a in range(3))
    grp_x, grp_y = [2 * v for v in sx], [v // 2 for v in sy]
    dev_y, dev_z = [8 * (v % 2) for v in sy], [2 * v + core for v in sz]
    along_x = [(grp_x[d] + grp_y[0], dev_y[0]) for d in range(4)]
    along_y = [(grp_x[0] + grp_y[d], dev_y[d]) for d in range(4)]
    mid1 = [tuple(jnp.where(even, a, b) for a, b in zip(along_x[d], along_y[d])) for d in range(4)]
    last1 = [tuple(jnp.where(even, a, b) for a, b in zip(along_y[d], along_x[d])) for d in range(4)]
    places = (
        (sz, sy, sx),
        ([jnp.where(even, a, b) for a, b in zip(sy, sx)], [jnp.where(even, a, b) for a, b in zip(sx, sy)], sz),
    )

    def chip_at(dx, dy, dz):
        return grp_x[dx] + grp_y[dy], dev_y[dy] + dev_z[dz]

    def peer(p, dl, dm, df):
        if not isinstance(p, int):
            return tuple(jnp.where(p == 0, a, b) for a, b in zip(peer(0, dl, dm, df), peer(1, dl, dm, df)))
        if p == 0:
            return chip_at(df, dm, dl)
        grp, dev = last1[dl] if dl else mid1[dm]
        return grp, dev + dev_z[df]

    def place(p):
        if isinstance(p, int):
            return tuple(axis[0] for axis in places[p])
        return tuple(jnp.where(p == 0, a[0], b[0]) for a, b in zip(*places))

    partner = device(me + 1 - 2 * core)

    def remote(src, dst, send, recv, to):
        return pltpu.make_async_remote_copy(
            src_ref=src, dst_ref=dst, send_sem=send, recv_sem=recv, device_id=to, device_id_type=MESH
        )

    own_mem = pltpu.make_async_copy(mem_ref, mraw.at[0], mem_sem)
    own_mem.start()
    small = (
        pltpu.make_async_copy(blab_hbm, blab_ref, in_sem.at[0]),
        pltpu.make_async_copy(batch_hbm, batch_ref, in_sem.at[1]),
        pltpu.make_async_copy(step_hbm, step_ref, in_sem.at[2]),
        pltpu.make_async_copy(mlab_ref, klraw.at[0], in_sem.at[3]),
        pltpu.make_async_copy(keep_ref, kpraw.at[0], in_sem.at[4]),
    )
    blocks = []
    for p in (0, 1):
        l, m, f = place(p)
        blocks.append(
            pltpu.make_async_copy(
                batch_hbm.at[pl.ds(p * ROWS, ROWS)], raw.at[p, l, m, f], in_sem.at[5 + p]
            )
        )
    for copy in (*small, *blocks):
        copy.start()

    barrier = pltpu.get_barrier_semaphore()
    def greet(p, dl, dm, df):
        pl.semaphore_signal(barrier, inc=1, device_id=peer(p, dl, dm, df), device_id_type=MESH)

    for j in OTHERS:
        greet(0, 0, j // 4, j % 4)
    for j in OTHERS:
        if j // 4 and j % 4:
            greet(1, 0, j // 4, j % 4)
    for off in (1, 2, 3):
        greet(0, off, 0, 0)
    pl.semaphore_signal(barrier, inc=1, device_id=partner, device_id_type=MESH)
    for copy in (*small, *blocks):
        copy.wait()
    for i in range(4):
        clab[:, 2 * ROWS * i : 2 * ROWS * (i + 1)] = blab_ref[...]
    for p in (0, 1):
        l, m, f = place(p)
        labs[p, l, m, f] = clab[...]
    pl.semaphore_wait(barrier, 28)

    def to_plane(p, j, back):
        dm, df = j // 4, j % 4
        l, middle, first = places[p][0][0], places[p][1], places[p][2]
        m, f = (middle[-dm % 4], first[-df % 4]) if back else (middle[0], first[0])
        rows, labels, to = raw.at[p, l, m, f], labs.at[p, l, m, f], peer(p, 0, dm, df)
        return (
            remote(rows, rows, pl_s.at[p, j - 1], pl_r.at[p, j - 1], to),
            remote(labels, labels, pll_s.at[p, j - 1], pll_r.at[p, j - 1], to),
        )

    def plane_start():
        for j in OTHERS:
            for p in (0, 1):
                for copy in to_plane(p, j, False):
                    copy.start()

    def plane_recv():
        for j in OTHERS:
            for p in (0, 1):
                for copy in to_plane(p, j, True):
                    copy.wait_recv()

    def plane_sent():
        for j in OTHERS:
            for p in (0, 1):
                for copy in to_plane(p, j, False):
                    copy.wait_send()

    def line_rows(p, off, back):
        l = place(p)[0]
        if back:
            l = (l + 4 - off) % 4
        rows = raw.at[p, l]
        return remote(rows, rows, ln_s.at[p, off // 2], ln_r.at[p, off // 2], peer(p, off, 0, 0))

    def line_labels(p, off, back):
        l = place(p)[0]
        if back:
            l = (l + 4 - off) % 4
        labels = labs.at[p, l]
        return remote(labels, labels, lnl_s.at[p, off - 1], lnl_r.at[p, off - 1], peer(p, off, 0, 0))

    def relay(p, off, back):
        l = place(p)[0]
        l = (l + (2 if back else 4 - off)) % 4
        half = raw.at[p, l, pl.ds(0 if off == 1 else 2, 2)]
        return remote(half, half, fw_s.at[p, off // 2], fw_r.at[p, off // 2], peer(p, off, 0, 0))

    halves = tuple(
        remote(
            mem_ref.at[pl.ds(h * 1024, 1024)], mraw.at[1, pl.ds(h * 1024, 1024)],
            pt_s.at[3 * h], pt_r.at[3 * h], partner,
        )
        for h in (0, 1)
    )
    swaps = (
        remote(mlab_ref, klraw.at[1], pt_s.at[1], pt_r.at[1], partner),
        remote(keep_ref, kpraw.at[1], pt_s.at[2], pt_r.at[2], partner),
    )
    for copy in swaps + halves:
        copy.start()
    plane_start()

    def normalize_memory(half, begin, end):
        def block(i, _):
            row = pl.multiple_of(i * 128, 128)
            kept = kpraw[half, :, pl.ds(row, 128)] > 0
            klab[:, pl.ds(pl.multiple_of(half * KEYS_DEV + row, 128), 128)] = jnp.where(
                kept, klraw[half, :, pl.ds(row, 128)], -1
            ).astype(F32)
            values = mraw[half, pl.ds(row, 128), :].astype(F32)
            scale = unit_scale(values) * column(jnp.where(kept, 1.0, 0.0))[:, 0:1]
            keys[pl.ds(pl.multiple_of(half * KEYS_DEV + row, 128), 128), :] = (values * scale).astype(BF16)
            return 0

        lax.fori_loop(begin, end, block, 0, unroll=8)

    own_mem.wait()
    normalize_memory(0, 0, 16)
    for copy in swaps:
        copy.wait_recv()
    halves[0].wait_recv()
    normalize_memory(1, 0, 8)
    halves[1].wait_recv()
    normalize_memory(1, 8, 16)
    plane_recv()
    for p in (1, 0):
        for off in (1, 3):
            line_rows(p, off, False).start()
        for off in (1, 3, 2):
            line_labels(p, off, False).start()

    dropped = float(KEYS) - jnp.sum(
        jnp.where(kpraw[...] > 0, 1.0, 0.0).reshape(2, KEYS_DEV), axis=(0, 1), keepdims=True
    )

    def prepare(p, l):
        values = raw[p, l].reshape(CHUNK, WIDTH).astype(F32)
        an[p, l] = (values * unit_scale(values)).astype(BF16)
        pages = labs[p, l].reshape(16, 128).astype(F32)
        wide = jnp.transpose(jnp.concatenate([pages] * 8, axis=0))
        mine = jnp.where(jnp.full((ROWS, 128), p, I32) == 0, wide[:ROWS], wide[ROWS : 2 * ROWS])
        for b in range(16):
            labc[p, l, pl.ds(b * ROWS, ROWS), :] = jnp.broadcast_to(mine[:, b : b + 1], (ROWS, 128))

    def score(p, l):
        s = lax.dot_general(
            an[p, l], keys[...], (((1,), (1,)), ((), ())), preferred_element_type=F32
        )
        labels = labc[p, l]
        all_sum = jnp.zeros((CHUNK, 128), F32)
        pos_sum = jnp.zeros((CHUNK, 128), F32)
        for j in range(0, KEYS, 128):
            same = labels == klab[:, j : j + 128]
            e = jnp.exp2(s[:, j : j + 128] * jnp.where(same, -2.0 * LOG2E, 50.0 * LOG2E))
            all_sum = all_sum + e
            pos_sum = pos_sum + jnp.where(same, e, 0.0)
            terms[p, l, :, j : j + 128] = e.astype(BF16)
        acc[0], acc[1] = all_sum, pos_sum
        for h in (0, 1):
            half = pl.ds(h * 128, 128)
            total = jnp.sum(jnp.transpose(acc[0, half, :]), axis=0, keepdims=True)
            pos = jnp.sum(jnp.transpose(acc[1, half, :]), axis=0, keepdims=True)
            sums[0, p, l, pl.ds(h, 1), :] = total - pos - dropped
            sums[0, p, l, pl.ds(2 + h, 1), :] = pos

    def visit(i, _):
        early_piece = jnp.logical_or(jnp.logical_or(i == 1, i == 2), jnp.logical_or(i == 3, i == 6))
        p = jnp.where(early_piece, 1, 0)
        off = jnp.where(i < 2, 0, jnp.where(i > 5, 2, jnp.where(i % 2 == 0, 1, 3)))
        here = (place(p)[0] + 4 - off) % 4

        @pl.when(jnp.logical_or(i == 2, i == 4))
        def _():
            for off in (1, 3):
                line_rows(p, off, True).wait_recv()
                relay(p, off, False).start()
                line_labels(p, off, True).wait_recv()

        @pl.when(i > 5)
        def _():
            for off in (1, 3):
                relay(p, off, True).wait_recv()
            line_labels(p, 2, True).wait_recv()

        prepare(p, here)
        score(p, here)
        return 0

    lax.fori_loop(0, 8, visit, 0)

    def part(p, l, weight):
        labels = labc[p, l]
        parts = []
        for j in range(0, KEYS, 128):
            same = labels == klab[:, j : j + 128]
            parts.append(weight(same, terms[p, l, :, j : j + 128].astype(F32)).astype(BF16))
        return jnp.dot(jnp.concatenate(parts, axis=1), keys[...], preferred_element_type=F32)

    def early(i):
        return i % 2, jnp.where(i == 2, 1, 2)

    def alone(i):
        p, off = early(i)
        l = (place(p)[0] + off) % 4
        pair[0, i] = part(p, l, lambda same, e: jnp.where(same, 0.0, e))
        pair[1, i] = part(p, l, lambda same, e: jnp.where(same, e, 0.0))

    def sums_plane(j):
        return remote(
            sums.at[0], sums_in.at[j - 1], as_s.at[j - 1], as_r.at[j - 1], chip_at(j % 4, j // 4, 0)
        )

    def sums_line(off):
        return remote(
            sums.at[1], sums_z.at[off - 1], az_s.at[off - 1], az_r.at[off - 1], chip_at(0, 0, off)
        )

    def add_up(i, _):
        @pl.when(i == 0)
        def _():
            for j in OTHERS:
                sums_plane(j).start()

        alone(i)

        @pl.when(i == 1)
        def _():
            for j in OTHERS:
                sums_plane(j).wait_recv()
            total = sums[0]
            for j in range(15):
                total = total + sums_in[j]
            sums[1] = total
            for off in (1, 3, 2):
                sums_line(off).start()

        return 0

    lax.fori_loop(0, 3, add_up, 0)
    for off in (1, 2, 3):
        sums_line(off).wait_recv()
    sums[2] = sums[1] + sums_z[0] + sums_z[1] + sums_z[2]

    def onward(p, off):
        side = off // 2
        return remote(
            sb1.at[p, 2, side], hb.at[p, side], h1_s.at[p, side], h1_r.at[p, side], peer(p, off, 0, 0)
        )

    def ring1(p, off, half):
        side = off // 2
        return remote(
            sb1.at[p, side, half], rb1.at[p, side, half],
            r1_s.at[p, side, half], r1_r.at[p, side, half], peer(p, off, 0, 0),
        )

    def dispatch(p, off, g):
        side = off // 2
        gr[p, side] = jnp.where(jnp.full((128, WIDTH), side, I32) == 0, g[:128], g[128:])
        sb1[p, side, 1 - side] = jnp.where(
            jnp.full((128, WIDTH), side, I32) == 0, g[128:], g[:128]
        ).astype(BF16)
        ring1(p, off, 1 - side).start()

    def complete(p, off):
        side = off // 2
        onward(p, off).wait_recv()
        sb1[p, side, side] = (gr[p, side] + hb[p, side].astype(F32)).astype(BF16)
        ring1(p, off, side).start()

    def weights(p, l):
        for h in (0, 1):
            half = pl.ds(h * 128, 128)
            den[p, l, 0, half, :] = column(1.0 + EXP_NEG * sums[2, p, l, pl.ds(h, 1), :])
            den[p, l, 1, half, :] = column(1.0 + EXP_POS * sums[2, p, l, pl.ds(2 + h, 1), :])
        return EXP_NEG / den[p, l, 0], -EXP_POS / den[p, l, 1]

    def ready(i):
        p, off = early(i)
        neg, pos = weights(p, (place(p)[0] + off) % 4)
        return jnp.concatenate(
            [
                pair[0, i, :, j : j + 128] * neg + pair[1, i, :, j : j + 128] * pos
                for j in range(0, WIDTH, 128)
            ],
            axis=1,
        )

    def push_early(p, _):
        sb1[p, 2] = ready(p).astype(BF16).reshape(2, 128, WIDTH)
        for off in (1, 3):
            onward(p, off).start()
        return 0

    lax.fori_loop(0, 2, push_early, 0)
    dispatch(0, 1, ready(2))

    def push(i, _):
        p, off = (i + 1) % 2, jnp.where(i == 0, 1, jnp.where(i < 3, 3, 0))
        l = (place(p)[0] + off) % 4
        neg, pos = weights(p, l)
        gown[p] = part(p, l, lambda same, e: e * jnp.where(same, pos, neg))

        @pl.when(i == 0)
        def _():
            dispatch(1, 1, gown[1])

        @pl.when(i == 1)
        def _():
            dispatch(0, 3, gown[0])
            complete(1, 1)

        @pl.when(i == 2)
        def _():
            dispatch(1, 3, gown[1])
            complete(0, 1)
            complete(0, 3)
            complete(1, 3)

        return 0

    lax.fori_loop(0, 5, push, 0)

    def ring2(p, j):
        dm, df = j // 4, j % 4
        block = places[p][1][dm] * 4 + places[p][2][df]
        return remote(
            sb2.at[p, block], rb2.at[p, j - 1], r2_s.at[p, j - 1], r2_r.at[p, j - 1], peer(p, 0, dm, df)
        )

    for p in (0, 1):
        for off in (1, 3):
            for half in (0, 1):
                ring1(p, off, half).wait_recv()
        g1[p] = (
            gown[p].reshape(2, 128, WIDTH) + rb1[p, 0].astype(F32) + rb1[p, 1].astype(F32)
        ).reshape(16, ROWS, WIDTH)
        sb2[p] = g1[p].astype(BF16)

        for j in OTHERS:
            ring2(p, j).start()

    step = step_ref[0]
    odd = step % 2
    mate = me + 1 - 2 * core
    asker = jnp.where(odd == 0, me, mate)
    block = ((asker + 1048576 - step) % 128) // 2
    wanted = jnp.full((ROWS, WIDTH), block, I32)
    wanted_row = jnp.full((1, 128), block, I32)

    def find(q, found):
        qx, qy, qz = q // 16, (q // 4) % 4, q % 4
        pick = wanted == q
        upper = an[0, qz, pl.ds(pl.multiple_of((qy * 4 + qx) * ROWS, ROWS), ROWS), :].astype(F32)
        ql, qm = jnp.where(core == 0, qy, qx), jnp.where(core == 0, qx, qy)
        lower = an[1, ql, pl.ds(pl.multiple_of((qm * 4 + qz) * ROWS, ROWS), ROWS), :].astype(F32)
        return (
            jnp.where(pick, upper, found[0]),
            jnp.where(pick, lower, found[1]),
            jnp.where(wanted_row == q, labs[0, qz, qy, qx], found[2]),
        )

    nothing = jnp.zeros((ROWS, WIDTH), F32)
    upper, lower, label_row = lax.fori_loop(
        0, 64, find, (nothing, nothing, jnp.zeros((1, 128), I32))
    )
    cand[pl.ds(0, ROWS), :] = upper.astype(BF16)
    cand[pl.ds(ROWS, ROWS), :] = lower.astype(BF16)
    clab[...] = label_row
    trade = (
        remote(cand, cand_in, bt_s.at[0], bt_r.at[0], partner),
        remote(clab, clab_in, bt_s.at[1], bt_r.at[1], partner),
    )
    for copy in trade:
        copy.start()

    for p in (0, 1):
        l, m, f = place(p)
        own = pl.ds(pl.multiple_of((m * 4 + f) * ROWS, ROWS), ROWS)
        mine = pl.ds(p * ROWS, ROWS)
        loss_ref[mine, :] = jnp.log(den[p, l, 1, own, :]) / 2.0 + jnp.log(den[p, l, 0, own, :]) / 50.0
    for p in (0, 1):
        l, m, f = place(p)

        for j in OTHERS:
            ring2(p, j).wait_recv()
        grad_unit = g1[p, m * 4 + f]
        for j in range(15):
            grad_unit = grad_unit + rb2[p, j].astype(F32)
        values = batch_ref[pl.ds(p * ROWS, ROWS), :].astype(F32)
        radius = jnp.sqrt(jnp.sum(values * values, axis=1, keepdims=True) + 1e-06)
        unit = values / radius
        along = jnp.sum(unit * grad_unit, axis=1, keepdims=True)
        grad_ref[pl.ds(p * ROWS, ROWS), :] = (grad_unit - unit * along) / radius

    for copy in trade:
        copy.wait_recv()
    keep_mine = jnp.full((2 * ROWS, WIDTH), odd, I32) == 0
    moved_ref[...] = jnp.where(keep_mine, cand[...].astype(F32), cand_in[...].astype(F32)).astype(BF16)
    mvlab_ref[...] = jnp.where(jnp.full((1, 128), odd, I32) == 0, clab[...], clab_in[...])

    for copy in swaps + halves + trade:
        copy.wait_send()
    plane_sent()

    for j in OTHERS:
        sums_plane(j).wait_send()
        for p in (0, 1):
            ring2(p, j).wait_send()
    for off in (1, 2, 3):
        sums_line(off).wait_send()
        for p in (0, 1):
            line_labels(p, off, False).wait_send()
    for off in (1, 3):
        for p in (0, 1):
            line_rows(p, off, False).wait_send()
            relay(p, off, False).wait_send()
            onward(p, off).wait_send()
            for half in (0, 1):
                ring1(p, off, half).wait_send()


def finish(
    step_hbm, grad_hbm, loss_hbm, moved_hbm, mvlab_hbm, mlab_hbm, mem_ref,
    grad_out, loss_out, lab_out, mem_out,
    step_ref, grad, loss_in, moved, mvlab, mlab, loss, labels, buf, small_sem, done_sem, sem_in, sem_out,
):
    pieces, size = buf.shape[0], buf.shape[1]
    loads = [
        pltpu.make_async_copy(mem_ref.at[pl.ds(i * size, size)], buf.at[i], sem_in.at[i])
        for i in range(pieces)
    ]
    stores = [
        pltpu.make_async_copy(buf.at[i], mem_out.at[pl.ds(i * size, size)], sem_out.at[i])
        for i in range(pieces)
    ]
    pairs = (
        (step_hbm, step_ref), (moved_hbm, moved), (mvlab_hbm, mvlab), (mlab_hbm, mlab),
        (loss_hbm, loss_in), (grad_hbm, grad),
    )
    small = [pltpu.make_async_copy(a, b, small_sem.at[i]) for i, (a, b) in enumerate(pairs)]
    results = [
        pltpu.make_async_copy(a, b, done_sem.at[i])
        for i, (a, b) in enumerate(((loss, loss_out), (labels, lab_out), (grad, grad_out)))
    ]
    for copy in (*small[:2], *loads, *small[2:]):
        copy.start()
    small[0].wait()
    small[1].wait()
    slot = step_ref[0] % SLOTS
    per_piece = size // (2 * ROWS)
    for i in range(pieces):
        loads[i].wait()

        @pl.when(slot // per_piece == i)
        def _():
            at = pl.multiple_of((slot % per_piece) * (2 * ROWS), 2 * ROWS)
            buf[i, pl.ds(at, 2 * ROWS), :] = moved[...]

        stores[i].start()
    for copy in small[2:]:
        copy.wait()
    results[2].start()
    rows = loss_in.shape[0]
    diagonal = lax.broadcasted_iota(I32, (rows, 128), 0) == lax.broadcasted_iota(I32, (rows, 128), 1)
    loss[...] = jnp.sum(jnp.where(diagonal, loss_in[...], 0.0), axis=0, keepdims=True)[:, :rows]
    results[0].start()
    lane = lax.broadcasted_iota(I32, (1, 128), 1) // (2 * ROWS)
    for i in range(KEYS_DEV // 128):
        here = pl.ds(i * 128, 128)
        labels[:, here] = jnp.where(
            lane + i * (64 // ROWS) == jnp.full((1, 128), slot, I32), mvlab[...], mlab[:, here]
        )
    results[1].start()
    for copy in (*stores, *results):
        copy.wait()


def per_device(batch_rows, batch_labels, memory, memory_labels, keep_bits, step_index):
    local_rows = batch_rows.shape[0]
    vmem, hbm = pl.BlockSpec(memory_space=pltpu.VMEM), pl.BlockSpec(memory_space=pl.ANY)
    dma = pltpu.SemaphoreType.DMA
    memory_labels_row = memory_labels.reshape(1, KEYS_DEV)
    grad, loss, moved, moved_labels = pl.pallas_call(
        kernel,
        out_shape=(
            jax.ShapeDtypeStruct((local_rows, WIDTH), F32),
            jax.ShapeDtypeStruct((local_rows, 128), F32),
            jax.ShapeDtypeStruct((local_rows, WIDTH), BF16),
            jax.ShapeDtypeStruct((1, 128), I32),
        ),
        in_specs=[hbm] * 6,
        out_specs=(vmem, vmem, vmem, vmem),
        scratch_shapes=[
            pltpu.SMEM((1,), I32),
            pltpu.VMEM((2 * ROWS, WIDTH), BF16),
            pltpu.VMEM((1, 2 * ROWS), I32),
            pltpu.VMEM((2, KEYS_DEV, WIDTH), BF16),
            pltpu.VMEM((2, 1, KEYS_DEV), I32),
            pltpu.VMEM((2, 1, KEYS_DEV), I32),
            pltpu.VMEM((KEYS, WIDTH), BF16),
            pltpu.VMEM((1, KEYS), F32),
            pltpu.VMEM((2, 4, 4, 4, ROWS, WIDTH), BF16),
            pltpu.VMEM((2, 4, 4, 4, 1, 128), I32),
            pltpu.VMEM((2, 4, CHUNK, WIDTH), BF16),
            pltpu.VMEM((2, 4, CHUNK, 128), F32),
            pltpu.VMEM((2, 4, CHUNK, KEYS), BF16),
            pltpu.VMEM((2, CHUNK, 128), F32),
            pltpu.VMEM((3, 2, 4, 4, 128), F32),
            pltpu.VMEM((15, 2, 4, 4, 128), F32),
            pltpu.VMEM((3, 2, 4, 4, 128), F32),
            pltpu.VMEM((2, 4, 2, CHUNK, 128), F32),
            pltpu.VMEM((2, 3, CHUNK, WIDTH), F32),
            pltpu.VMEM((2, CHUNK, WIDTH), F32),
            pltpu.VMEM((2, 3, 2, 128, WIDTH), BF16),
            pltpu.VMEM((2, 2, 2, 128, WIDTH), BF16),
            pltpu.VMEM((2, 2, 128, WIDTH), BF16),
            pltpu.VMEM((2, 2, 128, WIDTH), F32),
            pltpu.VMEM((2, 16, ROWS, WIDTH), F32),
            pltpu.VMEM((2, 16, ROWS, WIDTH), BF16),
            pltpu.VMEM((2, 15, ROWS, WIDTH), BF16),
            pltpu.VMEM((2 * ROWS, WIDTH), BF16),
            pltpu.VMEM((2 * ROWS, WIDTH), BF16),
            pltpu.VMEM((1, 128), I32),
            pltpu.VMEM((1, 128), I32),
            dma,
            dma((7,)),
            dma((2, 15)), dma((2, 15)), dma((2, 15)), dma((2, 15)),
            dma((2, 2)), dma((2, 2)), dma((2, 3)), dma((2, 3)), dma((2, 2)), dma((2, 2)),
            dma((15,)), dma((15,)), dma((3,)), dma((3,)),
            dma((2, 2)), dma((2, 2)), dma((2, 2, 2)), dma((2, 2, 2)), dma((2, 15)), dma((2, 15)),
            dma((4,)), dma((4,)), dma((2,)), dma((2,)),
        ],
        compiler_params=pltpu.CompilerParams(
            collective_id=0, has_side_effects=True, vmem_limit_bytes=60 * 1024 * 1024
        ),
        name="xbm",
    )(
        step_index,
        batch_rows,
        batch_labels.reshape(1, local_rows),
        memory_labels_row,
        keep_bits.reshape(1, KEYS_DEV),
        memory,
    )
    pieces = 4
    grad, loss_row, new_labels, new_memory = pl.pallas_call(
        finish,
        out_shape=(
            jax.ShapeDtypeStruct((local_rows, WIDTH), F32),
            jax.ShapeDtypeStruct((1, local_rows), F32),
            jax.ShapeDtypeStruct((1, KEYS_DEV), I32),
            jax.ShapeDtypeStruct((KEYS_DEV, WIDTH), BF16),
        ),
        in_specs=[hbm] * 7,
        out_specs=(hbm,) * 4,
        scratch_shapes=[
            pltpu.SMEM((1,), I32),
            pltpu.VMEM((local_rows, WIDTH), F32),
            pltpu.VMEM((local_rows, 128), F32),
            pltpu.VMEM((local_rows, WIDTH), BF16),
            pltpu.VMEM((1, 128), I32),
            pltpu.VMEM((1, KEYS_DEV), I32),
            pltpu.VMEM((1, local_rows), F32),
            pltpu.VMEM((1, KEYS_DEV), I32),
            pltpu.VMEM((pieces, KEYS_DEV // pieces, WIDTH), BF16),
            dma((6,)), dma((3,)), dma((pieces,)), dma((pieces,)),
        ],
        name="finish",
    )(step_index, grad, loss, moved, moved_labels, memory_labels_row, memory)
    return grad, loss_row.reshape(local_rows), new_memory, new_labels.reshape(KEYS_DEV)


def solution(mesh):
    rows = P(("grp", "dev"), None)
    flat = P(("grp", "dev"))
    return jax.shard_map(
        per_device,
        mesh=mesh,
        in_specs=(rows, flat, rows, flat, flat, P()),
        out_specs=(rows, flat, rows, flat),
        check_vma=False,
    )
```
